32 devices in a mesh: stream: 4 (over y, core), seq: 4 (over z), dp: 2 (over x).
Axes of the slice: x: 2, y: 2, z: 4, core: 2. Of those that a mesh axis runs over, the one named last changes fastest.
Arguments:
- video_query: bfloat16 [2048, 4096], P(('dp', 'seq'), 'stream'), parts along dimension 0, may hold values from -256 to 256
- video_key: bfloat16 [2048, 4096], P(('dp', 'seq'), 'stream'), parts along dimension 0, may hold values from -6 to 6
- video_value: bfloat16 [2048, 4096], P(('dp', 'seq'), 'stream'), parts along dimension 0, may hold values from -6 to 6
- video_keep: int32 [2048], P(('dp', 'seq')), parts along dimension 0, may hold values 0 or 1
- video_blocks: int32 [16, 8], P('dp'), parts along dimension 0, may hold values 0 or 1
- video_time: int32 [2048], P(('dp', 'seq')), parts along dimension 0, may hold values from 0 to 15, never falling along the last dimension, each value on 1 to 128 neighbouring positions
- audio_query: bfloat16 [1024, 2048], P(('dp', 'seq'), 'stream'), parts along dimension 0, may hold values from -256 to 256
- audio_key: bfloat16 [1024, 2048], P(('dp', 'seq'), 'stream'), parts along dimension 0, may hold values from -6 to 6
- audio_value: bfloat16 [1024, 2048], P(('dp', 'seq'), 'stream'), parts along dimension 0, may hold values from -6 to 6
- audio_keep: int32 [1024], P(('dp', 'seq')), parts along dimension 0, may hold values 0 or 1
- audio_time: int32 [1024], P(('dp', 'seq')), parts along dimension 0, may hold values from 0 to 15, never falling along the last dimension, each value on 1 to 64 neighbouring positions
- video_cross_query: bfloat16 [2048, 2048], P(('dp', 'seq'), 'stream'), parts along dimension 0, may hold values from -256 to 256
- audio_cross_key: bfloat16 [1024, 2048], P(('dp', 'seq'), 'stream'), parts along dimension 0, may hold values from -6 to 6
- audio_cross_value: bfloat16 [1024, 2048], P(('dp', 'seq'), 'stream'), parts along dimension 0, may hold values from -6 to 6
- audio_cross_query: bfloat16 [1024, 2048], P(('dp', 'seq'), 'stream'), parts along dimension 0, may hold values from -256 to 256
- video_cross_key: bfloat16 [2048, 2048], P(('dp', 'seq'), 'stream'), parts along dimension 0, may hold values from -6 to 6
- video_cross_value: bfloat16 [2048, 2048], P(('dp', 'seq'), 'stream'), parts along dimension 0, may hold values from -6 to 6
- video_out_w: bfloat16 [4096, 4096], P('stream'), may hold values from -0.125 to 0.125
- video_cross_w: bfloat16 [2048, 4096], P('stream'), may hold values from -0.1875 to 0.1875
- audio_out_w: bfloat16 [2048, 2048], P('stream'), may hold values from -0.1875 to 0.1875
- audio_cross_w: bfloat16 [2048, 2048], P('stream'), may hold values from -0.1875 to 0.1875
Outputs:
- video_update: bfloat16 [2048, 4096], P(('dp', 'seq'), 'stream'), parts along dimension 0
- audio_update: bfloat16 [1024, 2048], P(('dp', 'seq'), 'stream'), parts along dimension 0
The draws below stay inside these ranges and needn't reach their ends.
There are 2 independent parts, one for each index of `dp`. The reference program is written for one: setup_inputs(seed, part) draws one part's arguments, and reference() takes and returns one part's arrays. A program takes and returns all parts, laid end to end along the dimension named above; an argument that names none is the same for every part. Nothing has to cross between parts.
All inputs are finite; a program needn't handle non-finite values. No bound on the sum of `video_keep` or of `audio_keep` on one device may be relied on, other than what follows from the above.
Results may differ from the reference program's by a relative error of at most 0.015.
Values may be sent and summed in bfloat16 or wider, within the bound.
No kernel may reach another device: no remote copies, remote signals or barrier semaphores. Data moves between devices by JAX's collectives and lax.ppermute only.
A program may use at most 64 MiB of HBM per device.

```python
import math
import jax
import jax.numpy as jnp
import numpy as np
from jax import lax

DV = 4096
HV = 32
DA = 2048
HA = 32
BLOCK = 128
FRAMES = 16
WINDOW = 10
LV = 1024
LA = 512


def paired_draw(key, query_rows, key_rows, width):
    key_seed, query_seed = jax.random.split(key)
    key_part = jnp.clip(jax.random.normal(key_seed, (key_rows, width), jnp.float32), -6.0, 6.0)
    query_part = jnp.clip(jax.random.normal(query_seed, (query_rows, width), jnp.float32), -6.0, 6.0)
    return (query_part, key_part)


def draw_video_query(key, part):
    return paired_draw(jax.random.fold_in(key, 101), LV, LV, DV)[0].astype(jnp.bfloat16)


def draw_video_key(key, part):
    return paired_draw(jax.random.fold_in(key, 101), LV, LV, DV)[1].astype(jnp.bfloat16)


def draw_audio_query(key, part):
    return paired_draw(jax.random.fold_in(key, 102), LA, LA, DA)[0].astype(jnp.bfloat16)


def draw_audio_key(key, part):
    return paired_draw(jax.random.fold_in(key, 102), LA, LA, DA)[1].astype(jnp.bfloat16)


def draw_video_cross_query(key, part):
    return paired_draw(jax.random.fold_in(key, 103), LV, LA, DA)[0].astype(jnp.bfloat16)


def draw_audio_cross_key(key, part):
    return paired_draw(jax.random.fold_in(key, 103), LV, LA, DA)[1].astype(jnp.bfloat16)


def draw_audio_cross_query(key, part):
    return paired_draw(jax.random.fold_in(key, 104), LA, LV, DA)[0].astype(jnp.bfloat16)


def draw_video_cross_key(key, part):
    return paired_draw(jax.random.fold_in(key, 104), LA, LV, DA)[1].astype(jnp.bfloat16)


def plant(values, stream_key, smallest, top_value):
    shape = values.shape
    index_at = [jax.random.randint(jax.random.fold_in(stream_key, axis), (), 0, shape[axis]) for axis in range(len(shape))]
    values = values.at[tuple(index_at)].set(smallest)
    longest = shape.index(max(shape))
    index_at[longest] = (index_at[longest] + 1) % shape[longest]
    return values.at[tuple(index_at)].set(top_value)


def with_spikes(values, key, source, target, shards_of, factor):
    owner, partner = [(jnp.arange(values.shape[dim]) // (values.shape[dim] // shards_of)).reshape([-1 if axis == dim else 1 for axis in range(values.ndim)]) for dim in (source, target)]
    chosen = jax.random.permutation(key, shards_of)[partner]
    strong = (owner == chosen) | (owner == (partner + shards_of // 2) % shards_of)
    return jnp.where(strong, factor * values, values)


def levels(stream_key, dims, cuts, least, high):
    gain = 1.0
    for position, blocks in cuts:
        steps = jax.random.uniform(jax.random.fold_in(jax.random.fold_in(stream_key, 6), position), (blocks,), jnp.float32, least / len(cuts), high / len(cuts))
        gain = gain * jnp.repeat(jnp.exp(steps), dims[position] // blocks).reshape((-1,) + (1,) * (len(dims) - 1 - position))
    return gain


def split_up(amount, total, most, skew):
    loads = [(1 << 20) // math.isqrt(rank ** skew) + 1 for rank in range(2, amount + 1)]
    surplus, given = total - most - (amount - 1), [1] * (amount - 1)
    while surplus > 0:
        free = [i for i in range(amount - 1) if given[i] < most]
        pool, left = sum([loads[i] for i in free]), surplus
        for i in free:
            more = min(most - given[i], max(1, left * loads[i] // pool), surplus)
            given[i] = given[i] + more
            surplus = surplus - more
    return np.array([most] + given)


def uneven_parts(key, count, total, bound, skew):
    if count == 2:
        one = jax.random.randint(key, (), max(1, total - bound), min(bound, total - 1) + 1)
        return jnp.stack([one, total - one])
    sizes = jnp.asarray(split_up(count, total, bound, skew), jnp.int32)
    couples = (count - 1) // 2
    source_of, taker = sizes[1:1 + 2 * couples:2], sizes[2:2 + 2 * couples:2]
    room = jnp.minimum(source_of - 1, bound - taker)
    shifted = jax.random.randint(jax.random.fold_in(key, 1), (couples,), 0, 1 << 20) % (room + 1)
    sizes = sizes.at[1:1 + 2 * couples:2].set(source_of - shifted).at[2:2 + 2 * couples:2].set(taker + shifted)
    return sizes[jax.random.permutation(jax.random.fold_in(key, 2), count)]


def bell_draw(key, dims, scale, limit, cuts=(), held_as=jnp.bfloat16):
    level = levels(key, dims, cuts, -0.22, 0.18) if cuts else 1.0
    drawn = jax.random.normal(key, dims, jnp.float32) * scale * level
    return jnp.minimum(jnp.maximum(drawn, -limit), limit).astype(held_as)


def gaussian_with(rng, shape, scale, most, pieces, heavy, held_as=jnp.bfloat16):
    drawn = scale * jax.random.normal(rng, shape, jnp.float32)
    if pieces:
        drawn = drawn * levels(rng, shape, pieces, -0.22, 0.18)
    return jnp.clip(with_spikes(drawn, jax.random.fold_in(rng, 3), *heavy), -most, most).astype(held_as)


def setup_inputs(seed: int = 0, part: int = 0) -> dict:
    splits = jax.random.split(jax.random.key(seed), 22)
    own_keys = jax.random.split(jax.random.fold_in(splits[21], part), 22)
    video_query = draw_video_query(jax.random.fold_in(jax.random.fold_in(splits[21], part), 71), part)
    video_key = draw_video_key(jax.random.fold_in(jax.random.fold_in(splits[21], part), 71), part)
    video_value = bell_draw(own_keys[2], (LV, DV), 1.0, 6.0, ((0, 4), (1, 4)))
    video_keep = plant((jax.random.randint(own_keys[3], (LV,), 0, 4) < 3).astype(jnp.int32), jax.random.fold_in(own_keys[3], 1), 0, 1)
    video_blocks = plant((jax.random.randint(own_keys[4], (LV // BLOCK, LV // BLOCK), 0, 2) < 1).astype(jnp.int32), jax.random.fold_in(own_keys[4], 1), 0, 1)
    video_time = jnp.searchsorted(jnp.cumsum(uneven_parts(own_keys[5], FRAMES, LV, 2 * LV // FRAMES, 1)), jnp.arange(LV), side="right").astype(jnp.int32)
    audio_query = draw_audio_query(jax.random.fold_in(jax.random.fold_in(splits[21], part), 71), part)
    audio_key = draw_audio_key(jax.random.fold_in(jax.random.fold_in(splits[21], part), 71), part)
    audio_value = bell_draw(own_keys[8], (LA, DA), 1.0, 6.0, ((0, 4), (1, 4)))
    audio_keep = plant((jax.random.randint(own_keys[9], (LA,), 0, 4) < 3).astype(jnp.int32), jax.random.fold_in(own_keys[9], 1), 0, 1)
    audio_time = jnp.searchsorted(jnp.cumsum(uneven_parts(own_keys[10], FRAMES, LA, 2 * LA // FRAMES, 1)), jnp.arange(LA), side="right").astype(jnp.int32)
    video_cross_query = draw_video_cross_query(jax.random.fold_in(jax.random.fold_in(splits[21], part), 71), part)
    audio_cross_key = draw_audio_cross_key(jax.random.fold_in(jax.random.fold_in(splits[21], part), 71), part)
    audio_cross_value = bell_draw(own_keys[13], (LA, DA), 1.0, 6.0, ((0, 4), (1, 4)))
    audio_cross_query = draw_audio_cross_query(jax.random.fold_in(jax.random.fold_in(splits[21], part), 71), part)
    video_cross_key = draw_video_cross_key(jax.random.fold_in(jax.random.fold_in(splits[21], part), 71), part)
    video_cross_value = bell_draw(own_keys[16], (LV, DA), 1.0, 6.0, ((0, 4), (1, 4)))
    video_out_w = gaussian_with(splits[17], (DV, DV), DV ** -0.5, 0.125, ((0, 4),), (0, 1, 4, 2.0))
    video_cross_w = gaussian_with(splits[18], (DA, DV), DA ** -0.5, 0.1875, ((0, 4),), (0, 1, 4, 2.0))
    audio_out_w = gaussian_with(splits[19], (DA, DA), DA ** -0.5, 0.1875, ((0, 4),), (0, 1, 4, 2.0))
    audio_cross_w = gaussian_with(splits[20], (DA, DA), DA ** -0.5, 0.1875, ((0, 4),), (0, 1, 4, 2.0))
    return dict(video_query=video_query, video_key=video_key, video_value=video_value, video_keep=video_keep, video_blocks=video_blocks, video_time=video_time, audio_query=audio_query, audio_key=audio_key, audio_value=audio_value, audio_keep=audio_keep, audio_time=audio_time, video_cross_query=video_cross_query, audio_cross_key=audio_cross_key, audio_cross_value=audio_cross_value, audio_cross_query=audio_cross_query, video_cross_key=video_cross_key, video_cross_value=video_cross_value, video_out_w=video_out_w, video_cross_w=video_cross_w, audio_out_w=audio_out_w, audio_cross_w=audio_cross_w)


def attention(queries, key_rows, value_rows, allowed, head_size):
    head_count = queries.shape[1] // head_size

    def heads_of(matrix):
        return matrix.reshape(matrix.shape[0], head_count, head_size).transpose(1, 0, 2)

    def single(operands):
        query_head, key_head, value_head = operands
        scores = jnp.dot(query_head, key_head.T, preferred_element_type=jnp.float32) * (head_size ** -0.5)
        highest = jnp.max(jnp.where(allowed, scores, -1e30), axis=1)
        weights = jnp.where(allowed, jnp.exp(scores - highest[:, None]), 0.0)
        totals = jnp.sum(weights, axis=1)
        mixed = jnp.dot(weights.astype(jnp.bfloat16), value_head, preferred_element_type=jnp.float32)
        return mixed / totals[:, None]

    stacked = lax.map(single, (heads_of(queries), heads_of(key_rows), heads_of(value_rows)))
    return stacked.transpose(1, 0, 2).reshape(queries.shape[0], head_count * head_size).astype(jnp.bfloat16)


def reference(video_query, video_key, video_value, video_keep, video_blocks, video_time, audio_query, audio_key, audio_value, audio_keep, audio_time, video_cross_query, audio_cross_key, audio_cross_value, audio_cross_query, video_cross_key, video_cross_value, video_out_w, video_cross_w, audio_out_w, audio_cross_w):
    video_pos = jnp.arange(video_query.shape[0], dtype=jnp.int32)
    audio_pos = jnp.arange(audio_query.shape[0], dtype=jnp.int32)
    tile_ids = video_pos // BLOCK
    tiles = video_blocks[tile_ids][:, tile_ids] == 1
    video_allowed = (tiles & (video_keep[None, :] == 1)) | (video_pos[:, None] == video_pos[None, :])
    audio_allowed = (audio_keep[None, :] == 1) | (audio_pos[:, None] == audio_pos[None, :])
    cross_allowed = jnp.abs(video_time[:, None] - audio_time[None, :]) <= WINDOW
    video_size = DV // HV
    audio_size = DA // HA
    video_self = attention(video_query, video_key, video_value, video_allowed, video_size)
    video_cross = attention(video_cross_query, audio_cross_key, audio_cross_value, cross_allowed, audio_size)
    audio_self = attention(audio_query, audio_key, audio_value, audio_allowed, audio_size)
    audio_cross = attention(audio_cross_query, video_cross_key, video_cross_value, cross_allowed.T, audio_size)
    video_update = jnp.dot(video_self, video_out_w, preferred_element_type=jnp.float32) + jnp.dot(video_cross, video_cross_w, preferred_element_type=jnp.float32)
    audio_update = jnp.dot(audio_self, audio_out_w, preferred_element_type=jnp.float32) + jnp.dot(audio_cross, audio_cross_w, preferred_element_type=jnp.float32)
    return video_update.astype(jnp.bfloat16), audio_update.astype(jnp.bfloat16)
```

```python
import functools
import math

import jax
import jax.numpy as jnp
from jax import lax
from jax.experimental import pallas as pl
from jax.experimental.pallas import tpu as pltpu
from jax.sharding import PartitionSpec as P

HV = 32
HA = 32
BLOCK = 128
WINDOW = 10
LANES = 128
TILE = 16
NEG = -1e30
LOG2E = math.log2(math.e)
F32 = jnp.float32
BF16 = jnp.bfloat16
VMEM = pl.BlockSpec(memory_space=pltpu.VMEM)
SMEM = pl.BlockSpec(memory_space=pltpu.SMEM)


def swap(x, axis, count, distance):
    return lax.ppermute(x, axis, [(i, i ^ distance) for i in range(count)])


def far_first(count):
    return [j for j in range(count // 2, count)] + [j for j in range(1, count // 2)]


def gather_pairs(x, axis, count):
    blocks = {0: x}
    distance = count // 2
    while distance:
        blocks.update({j ^ distance: swap(blocks[j], axis, count, distance) for j in sorted(blocks)})
        distance //= 2
    return [blocks[j] for j in range(count)]


def cost(flops, size, exps=0):
    return pl.CostEstimate(flops=int(flops), bytes_accessed=int(size), transcendentals=int(exps))


def nt(a, b):
    return lax.dot_general(a, b, (((1,), (1,)), ((), ())), preferred_element_type=F32)


def mm(a, b):
    return jnp.dot(a, b, preferred_element_type=F32)


def column(row):
    parts = []
    eye = lax.broadcasted_iota(jnp.int32, (LANES, LANES), 0) == lax.broadcasted_iota(
        jnp.int32, (LANES, LANES), 1
    )
    for start in range(0, row.shape[1], LANES):
        piece = row[:, start : start + LANES]
        parts.append(jnp.sum(jnp.where(eye, piece, 0.0), axis=1, keepdims=True))
    return parts[0] if len(parts) == 1 else jnp.concatenate(parts, axis=0)


def flag_rows(width, keep, vtime, akeep, atime):
    def widen(row):
        row = row.astype(F32)
        gap = width - row.shape[1]
        return jnp.concatenate([row, jnp.zeros((1, gap), F32)], axis=1) if gap else row

    third = widen(jnp.concatenate([akeep.astype(F32), atime.astype(F32)], axis=1))
    index = lax.broadcasted_iota(jnp.int32, (TILE, width), 0)
    rows = jnp.where(index == 0, widen(keep), 0.0)
    rows = jnp.where(index == 1, widen(vtime), rows)
    rows = jnp.where(index == 2, third, rows)
    return rows.astype(BF16)


def pack_kernel(split, parts, *refs):
    arrays, flags, outs = refs[:parts], refs[parts : parts + 4], refs[parts + 4 :]
    rows = arrays[0].shape[0]
    width = arrays[0].shape[1] // split
    tail = flag_rows(width, *(f[...] for f in flags))
    me = lax.axis_index("seq") if split > 1 else 0
    for j, out in enumerate(outs):
        if split > 1:
            columns = pl.ds(pl.multiple_of((me ^ j) * width, width), width)
        else:
            columns = slice(None)
        for i, array in enumerate(arrays):
            out[i * rows : (i + 1) * rows, :] = array[:, columns]
        out[parts * rows :, :] = tail


def pack(arrays, flags, split):
    rows, width = arrays[0].shape
    width //= split
    total = len(arrays) * rows + TILE
    return pl.pallas_call(
        functools.partial(pack_kernel, split, len(arrays)),
        out_shape=[jax.ShapeDtypeStruct((total, width), BF16)] * split,
        in_specs=[VMEM] * (len(arrays) + 4),
        out_specs=[VMEM] * split,
        cost_estimate=cost(0, 4 * total * width * split),
        name="pack_video",
    )(*arrays, *(f.reshape(1, -1) for f in flags))


def video_self_kernel(count, queries_own, scale, key_at, *refs):
    blocks = refs[0]
    packs = refs[1 : 1 + count]
    n_q = 1 if queries_own else count
    query_refs = refs[1 + count : 2 + count] if queries_own else packs
    refs = refs[(2 if queries_own else 1) + count :]
    outs, (k_all, v_all, keep_all, q_all, o_all) = refs[:n_q], refs[n_q:]
    width = k_all.shape[1]
    rows = q_all.shape[0] // n_q
    size = BLOCK
    tiles = rows // BLOCK
    me = lax.axis_index("seq")
    for j in range(count):
        base = key_at * rows
        k_all[j * rows : (j + 1) * rows, :] = packs[j][base : base + rows, :]
        v_all[j * rows : (j + 1) * rows, :] = packs[j][base + rows : base + 2 * rows, :]
        tail = packs[j][base + 2 * rows :, :].astype(F32)
        keep_all[j * 8 : (j + 1) * 8, :] = jnp.broadcast_to(tail[0:1, :rows], (8, rows))
    for a in range(n_q):
        q_all[a * rows : (a + 1) * rows, :] = query_refs[a][0:rows, :]
    eye = lax.broadcasted_iota(jnp.int32, (BLOCK, BLOCK), 0) == lax.broadcasted_iota(
        jnp.int32, (BLOCK, BLOCK), 1
    )

    def body(a, carry):
        for t in range(tiles):
            tile_row = (me ^ a) * tiles + t
            bias = []
            for b in range(count):
                near = a ^ b
                keep = keep_all[pl.ds(pl.multiple_of(near * 8, 8), 8), :][0:1, :]
                for u in range(tiles):
                    seen = blocks[tile_row, (me ^ near) * tiles + u].astype(F32)
                    piece = keep[:, u * BLOCK : (u + 1) * BLOCK]
                    bias.append(jnp.where(piece * seen > 0.5, 0.0, NEG))
            at = pl.ds(pl.multiple_of(a * rows + t * BLOCK, BLOCK), BLOCK)
            for h in range(width // size):
                lanes = slice(h * size, (h + 1) * size)
                query = q_all[at, lanes]
                scores = []
                for b in range(count):
                    span = pl.ds(pl.multiple_of((a ^ b) * rows, rows), rows)
                    part = nt(query, k_all[span, lanes]) * scale
                    for u in range(tiles):
                        piece = part[:, u * BLOCK : (u + 1) * BLOCK]
                        masked = piece + bias[b * tiles + u]
                        if b == 0 and u == t:
                            masked = jnp.where(eye, piece, masked)
                        scores.append(masked)
                scores = jnp.concatenate(scores, axis=1)
                top = jnp.max(scores, axis=1, keepdims=True)
                weights = jnp.exp2(scores - top)
                total = jnp.sum(weights, axis=1, keepdims=True)
                weights = weights.astype(BF16)
                mixed = None
                for b in range(count):
                    span = pl.ds(pl.multiple_of((a ^ b) * rows, rows), rows)
                    part = mm(weights[:, b * rows : (b + 1) * rows], v_all[span, lanes])
                    mixed = part if mixed is None else mixed + part
                o_all[at, lanes] = (mixed / total).astype(BF16)
        return carry

    lax.fori_loop(0, n_q, body, 0)
    for a in range(n_q):
        outs[a][...] = o_all[a * rows : (a + 1) * rows, :]


def video_self_attention(blocks, packs, rows, own=None):
    count, width = len(packs), packs[0].shape[1]
    n_q = count if own is None else 1
    key_at = 1 if own is None else 0
    extra = [] if own is None else [own]
    keys = count * rows
    return pl.pallas_call(
        functools.partial(
            video_self_kernel, count, own is not None, BLOCK ** (-0.5) * LOG2E, key_at
        ),
        out_shape=[jax.ShapeDtypeStruct((rows, width), BF16)] * n_q,
        in_specs=[SMEM] + [VMEM] * (count + len(extra)),
        out_specs=[VMEM] * n_q,
        scratch_shapes=[
            pltpu.VMEM((keys, width), BF16),
            pltpu.VMEM((keys, width), BF16),
            pltpu.VMEM((count * 8, rows), F32),
            pltpu.VMEM((n_q * rows, width), BF16),
            pltpu.VMEM((n_q * rows, width), BF16),
        ],
        cost_estimate=cost(
            8 * n_q * rows * keys * width, 8 * keys * width, n_q * rows * keys * width // BLOCK
        ),
        name="video_self",
    )(blocks, *packs, *extra)


def attend_pair(query, key, value, bias, scale, size):
    lane = lax.broadcasted_iota(jnp.int32, (1, LANES), 1)
    outs, stats = [], []
    for half in range(LANES // size):
        mine = (lane >= half * size) & (lane < (half + 1) * size)
        part = jnp.where(mine, query, jnp.zeros_like(query))
        scores = nt(part, key) * scale + bias
        top = jnp.max(scores, axis=1, keepdims=True)
        weights = jnp.exp2(scores - top)
        total = jnp.sum(weights, axis=1, keepdims=True)
        mixed = mm(weights.astype(BF16), value) / total
        outs.append(jnp.where(mine, mixed, 0.0))
        stats.append((top, total))
    return functools.reduce(jnp.add, outs), stats


def bias_of(allowed):
    return jnp.where(allowed, 0.0, NEG)


def near_times(query_column, key_row):
    return bias_of(jnp.abs(query_column - key_row) <= WINDOW)


def own_query_kernel(kind, count, size, *refs):
    query, gathered, flags = refs[0], refs[1 : 1 + count], refs[1 + count : 1 + 2 * count]
    out, k_all, v_all, bias = refs[1 + 2 * count :]
    keys = k_all.shape[0] // count
    rows, width = query.shape
    tails = [f[...].astype(F32) for f in flags]
    for j in range(count):
        span = slice(j * keys, (j + 1) * keys)
        k_all[span, :] = gathered[j][0:keys, :]
        v_all[span, :] = gathered[j][keys : 2 * keys, :]
        if kind == "cross":
            bias[:, span] = near_times(
                column(tails[0][1:2, :rows]), tails[j][2:3, keys : 2 * keys]
            )
        else:
            mask = jnp.broadcast_to(tails[j][2:3, :keys], (rows, keys)) > 0.5
            if j == 0:
                mask = mask | (
                    lax.broadcasted_iota(jnp.int32, (rows, keys), 0)
                    == lax.broadcasted_iota(jnp.int32, (rows, keys), 1)
                )
            bias[:, span] = bias_of(mask)

    def body(pair, carry):
        lanes = pl.ds(pl.multiple_of(pair * LANES, LANES), LANES)
        mixed, _ = attend_pair(
            query[:, lanes], k_all[:, lanes], v_all[:, lanes], bias[...], size**-0.5 * LOG2E, size
        )
        out[:, lanes] = mixed.astype(BF16)
        return carry

    lax.fori_loop(0, width // LANES, body, 0)


def own_query_attention(kind, query, gathered, packs, keys, size):
    count = len(gathered)
    rows, width = query.shape
    tail = pl.BlockSpec((TILE, packs[0].shape[1]), lambda i: (packs[0].shape[0] // TILE - 1, 0))
    whole = lambda a: pl.BlockSpec(a.shape, lambda i: (0, 0))
    return pl.pallas_call(
        functools.partial(own_query_kernel, kind, count, size),
        grid=(1,),
        out_shape=jax.ShapeDtypeStruct((rows, width), BF16),
        in_specs=[whole(query)] + [whole(g) for g in gathered] + [tail] * count,
        out_specs=whole(query),
        scratch_shapes=[
            pltpu.VMEM((count * keys, width), BF16),
            pltpu.VMEM((count * keys, width), BF16),
            pltpu.VMEM((rows, count * keys), F32),
        ],
        cost_estimate=cost(
            8 * rows * count * keys * width,
            2 * count * gathered[0].size + 4 * query.size,
            rows * count * keys * width // size,
        ),
        name="own_query_" + kind,
    )(query, *gathered, *packs)


def split_three(x):
    high = x.astype(BF16)
    rest = x - high.astype(F32)
    middle = rest.astype(BF16)
    low = (rest - middle.astype(F32)).astype(BF16)
    return high, middle, low


def stat_layout(width, rows):
    across = min(3, width // rows)
    return across, -(-3 // across)


def own_key_kernel(count, size, *refs):
    key, value, gathered = refs[0], refs[1], refs[2 : 2 + count]
    flags, outs = refs[2 + count : 2 + 2 * count], refs[2 + 2 * count : 2 + 3 * count]
    q_all, bias, o_all, sums = refs[2 + 3 * count :]
    keys, width = key.shape
    rows = q_all.shape[0] // count
    tails = [f[...].astype(F32) for f in flags]
    for j in range(count):
        span = slice(j * rows, (j + 1) * rows)
        q_all[span, :] = gathered[j][2 * rows : 3 * rows, :]
        bias[span, :] = near_times(
            column(tails[j][2:3, rows : 2 * rows]), tails[0][1:2, :keys]
        )
    sums[...] = jnp.zeros_like(sums)
    lane = lax.broadcasted_iota(jnp.int32, (1, LANES), 1)
    per = LANES // size

    def body(pair, carry):
        lanes = pl.ds(pl.multiple_of(pair * LANES, LANES), LANES)
        mixed, stats = attend_pair(
            q_all[:, lanes], key[:, lanes], value[:, lanes], bias[...], size**-0.5 * LOG2E, size
        )
        o_all[:, lanes] = mixed.astype(BF16)
        tile = sums[...]
        for half, (top, total) in enumerate(stats):
            tile = jnp.where(lane == pair * per + half, top + jnp.log2(total), tile)
        sums[...] = tile
        return carry

    lax.fori_loop(0, width // LANES, body, 0)
    across, down = stat_layout(width, rows)
    for j in range(count):
        outs[j][0:rows, :] = o_all[j * rows : (j + 1) * rows, :]
        flat = sums[j * rows : (j + 1) * rows, :].T[0:TILE, :]
        parts = split_three(flat)
        for i in range(down):
            pieces = list(parts[i * across : (i + 1) * across])
            gap = width - len(pieces) * rows
            if gap:
                pieces.append(jnp.zeros((TILE, gap), BF16))
            block = pieces[0] if len(pieces) == 1 else jnp.concatenate(pieces, axis=1)
            outs[j][rows + i * TILE : rows + (i + 1) * TILE, :] = block


def own_key_attention(key, value, gathered, packs, rows, size):
    count = len(gathered)
    keys, width = key.shape
    tail = pl.BlockSpec((TILE, packs[0].shape[1]), lambda i: (packs[0].shape[0] // TILE - 1, 0))
    whole = lambda a: pl.BlockSpec(a.shape, lambda i: (0, 0))
    out = jax.ShapeDtypeStruct((rows + TILE * stat_layout(width, rows)[1], width), BF16)
    return pl.pallas_call(
        functools.partial(own_key_kernel, count, size),
        grid=(1,),
        out_shape=[out] * count,
        in_specs=[whole(key), whole(value)] + [whole(g) for g in gathered] + [tail] * count,
        out_specs=[whole(out)] * count,
        scratch_shapes=[
            pltpu.VMEM((count * rows, width), BF16),
            pltpu.VMEM((count * rows, keys), F32),
            pltpu.VMEM((count * rows, width), BF16),
            pltpu.VMEM((count * rows, LANES), F32),
        ],
        cost_estimate=cost(
            8 * rows * count * keys * width,
            2 * count * (gathered[0].size + 2 * rows * width),
            rows * count * keys * width // size,
        ),
        name="own_key",
    )(key, value, *gathered, *packs)


def video_project_kernel(count, ids, *refs):
    parts, cross, w_self, w_cross, out = refs[:count], *refs[count:]
    me = lax.axis_index("seq") if count > 1 else 0
    total = mm(cross[...], w_cross[...])
    depth = parts[0].shape[1]
    for j in range(count):
        span = pl.ds(pl.multiple_of((me ^ j) * depth, depth), depth)
        total = total + mm(parts[j][...], w_self[span, :])
    out[0] = total.astype(out.dtype)


def audio_project_kernel(count, size, ids, own, *refs):
    parts, w_self, w_cross, out, merged = refs[:count], *refs[count:]
    rows, width = own.shape

    @pl.when(pl.program_id(0) == 0)
    def _():
        across, down = stat_layout(width, rows)
        sums = []
        for part in parts:
            pieces = []
            for i in range(3):
                line = part[rows + (i // across) * TILE : rows + (i // across + 1) * TILE, :]
                at = (i % across) * rows
                pieces.append(line[:, at : at + rows].astype(F32))
            sums.append(pieces[0] + pieces[1] + pieces[2])
        top = functools.reduce(jnp.maximum, sums)
        shares = [jnp.exp2(s - top) for s in sums]
        total = functools.reduce(jnp.add, shares)
        filler = jnp.zeros((LANES - TILE, rows), F32)
        shares = [jnp.concatenate([s / total, filler], axis=0).T for s in shares]
        lane = lax.broadcasted_iota(jnp.int32, (1, LANES), 1)
        per = LANES // size
        for pair in range(width // LANES):
            lanes = slice(pair * LANES, (pair + 1) * LANES)
            mixed = None
            for share, part in zip(shares, parts):
                factor = share[:, pair * per : pair * per + 1]
                for half in range(1, per):
                    at = pair * per + half
                    factor = jnp.where(lane >= half * size, share[:, at : at + 1], factor)
                term = factor * part[0:rows, lanes].astype(F32)
                mixed = term if mixed is None else mixed + term
            merged[:, lanes] = mixed.astype(BF16)

    out[0] = (mm(own[...], w_self[...]) + mm(merged[...], w_cross[...])).astype(out.dtype)


def project(kernel, ids, operands, weights, rows, columns, dtype, scratch, name):
    whole = lambda a: pl.BlockSpec(a.shape, lambda i, ids: (0, 0))
    block = lambda w: pl.BlockSpec((w.shape[0], columns), lambda i, ids: (0, ids[i]))
    steps = ids.shape[0]
    depth = sum(w.shape[0] for w in weights)
    return pl.pallas_call(
        kernel,
        grid_spec=pltpu.PrefetchScalarGridSpec(
            num_scalar_prefetch=1,
            grid=(steps,),
            in_specs=[whole(a) for a in operands] + [block(w) for w in weights],
            out_specs=pl.BlockSpec((1, rows, columns), lambda i, ids: (i, 0, 0)),
            scratch_shapes=scratch,
        ),
        out_shape=jax.ShapeDtypeStruct((steps, rows, columns), dtype),
        cost_estimate=cost(
            2 * rows * depth * columns * steps, 2 * depth * columns * steps + 4 * rows * columns * steps
        ),
        name=name,
    )(ids, *operands, *weights)


def project_and_scatter(kernel, operands, weights, rows, scratch, name, shards):
    columns = weights[0].shape[1] // shards
    me = lax.axis_index("stream")
    relative = jnp.arange(shards // 2, dtype=jnp.int32) * 2
    call = lambda ids, dtype: project(
        kernel, ids, operands, weights, rows, columns, dtype, scratch, name
    )
    sent = call(me ^ (relative + 1), BF16)
    arrived = swap(sent, "stream", shards, 1)
    kept = call(me ^ relative, F32)
    sums = [kept[i] + arrived[i].astype(F32) for i in range(shards // 2)]
    distance = 2
    while len(sums) > 1:
        arrived = [swap(s.astype(BF16), "stream", shards, distance) for s in sums[1::2]]
        sums = [s + a.astype(F32) for s, a in zip(sums[0::2], arrived)]
        distance *= 2
    return sums[0].astype(BF16)


def shards(
    count,
    streams,
    video_query,
    video_key,
    video_value,
    video_keep,
    video_blocks,
    video_time,
    audio_query,
    audio_key,
    audio_value,
    audio_keep,
    audio_time,
    video_cross_query,
    audio_cross_key,
    audio_cross_value,
    audio_cross_query,
    video_cross_key,
    video_cross_value,
    video_out_w,
    video_cross_w,
    audio_out_w,
    audio_cross_w,
):
    rows, audio_rows = video_query.shape[0], audio_query.shape[0]
    audio_size = audio_cross_w.shape[1] // HA
    flags = (video_keep, video_time, audio_keep, audio_time)
    by_heads = (video_query.shape[1] // BLOCK) % count == 0
    if by_heads:
        packs = pack([video_query, video_key, video_value], flags, count)
        packs = [packs[0]] + [
            got for _, got in sorted((j, swap(packs[j], "seq", count, j)) for j in far_first(count))
        ]
    else:
        packs = gather_pairs(pack([video_key, video_value], flags, 1)[0], "seq", count)
    cross_keys = gather_pairs(
        jnp.concatenate([audio_cross_key, audio_cross_value], axis=0), "seq", count
    )
    if by_heads:
        mixed = video_self_attention(video_blocks, packs, rows)
        video_self = [mixed[0]] + [
            got for _, got in sorted((j, swap(mixed[j], "seq", count, j)) for j in far_first(count))
        ]
    else:
        video_self = video_self_attention(video_blocks, packs, rows, video_query)
    audio_all = gather_pairs(
        jnp.concatenate([audio_key, audio_value, audio_cross_query], axis=0), "seq", count
    )
    video_cross = own_query_attention(
        "cross", video_cross_query, cross_keys, packs, audio_rows, audio_size
    )
    partial = own_key_attention(
        video_cross_key, video_cross_value, audio_all, packs, audio_rows, audio_size
    )
    partial = [partial[0]] + [
        got for _, got in sorted((j, swap(partial[j], "seq", count, j)) for j in far_first(count))
    ]
    audio_self = own_query_attention("self", audio_query, audio_all, packs, audio_rows, audio_size)
    video_update = project_and_scatter(
        functools.partial(video_project_kernel, len(video_self)),
        [*video_self, video_cross],
        [video_out_w, video_cross_w],
        rows,
        [],
        "video_project",
        streams,
    )
    audio_update = project_and_scatter(
        functools.partial(audio_project_kernel, count, audio_size),
        [audio_self, *partial],
        [audio_out_w, audio_cross_w],
        audio_rows,
        [pltpu.VMEM(audio_self.shape, BF16)],
        "audio_project",
        streams,
    )
    return video_update, audio_update


def solution(mesh):
    tokens = P(("dp", "seq"))
    matrix = P(("dp", "seq"), "stream")
    weight = P("stream", None)
    return jax.shard_map(
        functools.partial(shards, mesh.shape["seq"], mesh.shape["stream"]),
        mesh=mesh,
        in_specs=(
            matrix,
            matrix,
            matrix,
            tokens,
            P("dp", None),
            tokens,
            matrix,
            matrix,
            matrix,
            tokens,
            tokens,
            matrix,
            matrix,
            matrix,
            matrix,
            matrix,
            matrix,
            weight,
            weight,
            weight,
            weight,
        ),
        out_specs=(matrix, matrix),
        check_vma=False,
    )
```

```python
import functools
import math

import jax
import jax.numpy as jnp
from jax import lax
from jax.experimental import pallas as pl
from jax.experimental.pallas import tpu as pltpu
from jax.sharding import PartitionSpec as P

HA = 32
BLOCK = 128
WINDOW = 10
LANES = 128
TILE = 16
NEG = -1e30
LOG2E = math.log2(math.e)
F32 = jnp.float32
BF16 = jnp.bfloat16
VMEM = pl.BlockSpec(memory_space=pltpu.VMEM)
SMEM = pl.BlockSpec(memory_space=pltpu.SMEM)
HBM = pl.BlockSpec(memory_space=pltpu.HBM)
MIB = 1 << 20


def swap(x, axis, count, distance):
    return lax.ppermute(x, axis, [(i, i ^ distance) for i in range(count)])


def far_first(count):
    return [*range(count // 2, count), *range(1, count // 2)]


def exchange(pieces, axis, count):
    arrived = {j: swap(pieces[j], axis, count, j) for j in far_first(count)}
    return [pieces[0]] + [arrived[j] for j in range(1, count)]


def gather_pairs(x, axis, count):
    blocks = {0: x}
    distance = count // 2
    while distance:
        for j in sorted(blocks):
            blocks[j ^ distance] = swap(blocks[j], axis, count, distance)
        distance //= 2
    return [blocks[j] for j in range(count)]


def call(kernel, operands, outs, scratch, work, specs=None, sems=()):
    blocked = [a for a, spec in zip(operands, specs or [VMEM] * len(operands)) if spec is not HBM]
    size = sum(a.size * a.dtype.itemsize for a in [*blocked, *outs])
    held = sum(math.prod(s.shape) * jnp.dtype(s.dtype).itemsize for s in scratch)
    flops, exps = work
    return pl.pallas_call(
        kernel,
        out_shape=outs,
        in_specs=specs or [VMEM] * len(operands),
        out_specs=[VMEM] * len(outs),
        scratch_shapes=[*scratch, *sems],
        compiler_params=pltpu.CompilerParams(vmem_limit_bytes=size + held + 8 * MIB),
        cost_estimate=pl.CostEstimate(
            flops=int(flops), bytes_accessed=int(size), transcendentals=int(exps)
        ),
    )(*operands)


def shape(*dims, dtype=BF16):
    return jax.ShapeDtypeStruct(dims, dtype)


def nt(a, b):
    return lax.dot_general(a, b, (((1,), (1,)), ((), ())), preferred_element_type=F32)


def mm(a, b):
    return jnp.dot(a, b, preferred_element_type=F32)


def join(parts, axis):
    return parts[0] if len(parts) == 1 else jnp.concatenate(parts, axis=axis)


def square_eye():
    return lax.broadcasted_iota(jnp.int32, (LANES, LANES), 0) == lax.broadcasted_iota(
        jnp.int32, (LANES, LANES), 1
    )


def column(row):
    eye, parts = square_eye(), []
    for start in range(0, row.shape[1], LANES):
        piece = row[:, start : start + LANES]
        parts.append(jnp.sum(jnp.where(eye, piece, 0.0), axis=1, keepdims=True))
    return join(parts, 0)


def bias_of(allowed):
    return jnp.where(allowed, 0.0, NEG)


def near_times(query_column, key_row):
    return bias_of(jnp.abs(query_column - key_row) <= WINDOW)


def flag_tile(flags, width):
    index = lax.broadcasted_iota(jnp.int32, (TILE, LANES), 0)
    tile = jnp.zeros((TILE, LANES), F32)
    at = 0
    for flag in flags:
        values = flag[...].astype(F32)
        for start in range(0, values.shape[1], LANES):
            tile = jnp.where(index == at, values[:, start : start + LANES], tile)
            at += 1
    gap = width - LANES
    return join([tile] + ([jnp.zeros((TILE, gap), F32)] if gap else []), 1).astype(BF16)


def flag_row(tile, which, rows, audio_rows):
    counts = [rows // LANES, rows // LANES, audio_rows // LANES, audio_rows // LANES]
    at = sum(counts[:which])
    return join([tile[i : i + 1, :] for i in range(at, at + counts[which])], 1)


KEEP, TIME, AUDIO_KEEP, AUDIO_TIME = range(4)


def pack_kernel(groups, n_flags, *refs):
    n_in = sum(len(layout) for layout, _, _ in groups)
    inputs, flags, rest = refs[:n_in], refs[n_in : n_in + n_flags], refs[n_in + n_flags :]
    n_out = sum(len(places) for _, places, _ in groups)
    outs, held, sems, flag_sems = rest[:n_out], rest[n_out:-2], rest[-2], rest[-1]
    me = lax.axis_index("seq")
    loads = [pltpu.make_async_copy(*pair, flag_sems.at[i]) for i, pair in enumerate(zip(flags, held))]
    copies = []
    first_in = first_out = 0
    for layout, places, parts in groups:
        for out, j in zip(outs[first_out:], places):
            for array, (row, lane) in zip(inputs[first_in:], layout):
                rows, width = array.shape[0], array.shape[1] // parts
                columns = slice(None)
                if parts > 1:
                    part = (me ^ j) & (parts - 1)
                    columns = pl.ds(pl.multiple_of(part * width, width), width)
                target = out.at[row : row + rows, lane : lane + width]
                copies.append(
                    pltpu.make_async_copy(array.at[:, columns], target, sems.at[len(copies)])
                )
        first_in, first_out = first_in + len(layout), first_out + len(places)
    for copy in loads + copies:
        copy.start()
    if n_flags:
        for copy in loads:
            copy.wait()
        tile = flag_tile(held, outs[0].shape[1])
        for out, _ in zip(outs, groups[0][1]):
            out[out.shape[0] - TILE :, :] = tile
    for copy in copies:
        copy.wait()


def in_hbm(array):
    return pltpu.with_memory_space_constraint(array, pltpu.HBM)


def pack(groups, flags=()):
    outs, layout, arrays = [], [], []
    for placed, places, parts in groups:
        rows = max(row + a.shape[0] for a, row, _ in placed)
        rows += TILE if flags and not outs else 0
        width = max(lane + a.shape[1] // parts for a, _, lane in placed)
        outs += [shape(rows, width, dtype=placed[0][0].dtype)] * len(places)
        layout.append(([(row, lane) for _, row, lane in placed], list(places), parts))
        arrays += [a for a, _, _ in placed]
    operands = [in_hbm(a) for a in arrays] + [in_hbm(f.reshape(1, -1)) for f in flags]
    copies = sum(len(spots) * len(places) for spots, places, _ in layout)
    got = call(
        functools.partial(pack_kernel, layout, len(flags)),
        operands,
        outs,
        [pltpu.VMEM((1, f.shape[0]), jnp.int32) for f in flags],
        (0, 0),
        [HBM] * len(operands),
        [pltpu.SemaphoreType.DMA((copies,)), pltpu.SemaphoreType.DMA((max(1, len(flags)),))],
    )
    split_up, at = [], 0
    for _, places, _ in groups:
        split_up.append(got[at : at + len(places)])
        at += len(places)
    return split_up


def below(*arrays):
    placed, row = [], 0
    for array in arrays:
        placed.append((array, row, 0))
        row += array.shape[0]
    return placed


def video_self_kernel(count, chosen, with_query, audio_rows, scale, *refs):
    blocks, packs = refs[0], refs[1 : 1 + count]
    query_refs = [refs[1 + count]] if with_query else [packs[a] for a in chosen]
    refs = refs[(2 if with_query else 1) + count :]
    n_q, first = len(query_refs), chosen[0]
    flags, outs, (q_all, k_all, v_all, o_all) = refs[0], refs[1 : 1 + n_q], refs[1 + n_q :]
    rows, width = q_all.shape[0] // n_q, q_all.shape[1]
    tiles = rows // BLOCK
    me = lax.axis_index("seq")
    at = 0 if with_query else rows
    for j in range(count):
        k_all[j * rows : (j + 1) * rows, :] = packs[j][at : at + rows, :]
        v_all[j * rows : (j + 1) * rows, :] = packs[j][at + rows : at + 2 * rows, :]
        flags[j * TILE : (j + 1) * TILE, :] = packs[j][at + 2 * rows :, :LANES].astype(F32)
    for a in range(n_q):
        q_all[a * rows : (a + 1) * rows, :] = query_refs[a][0:rows, :]
    eye = square_eye()

    def body(i, carry):
        a = first + i
        bias = []
        for b in range(count):
            near = a ^ b
            tile = flags[pl.ds(pl.multiple_of(near * TILE, TILE), TILE), :]
            keep = flag_row(tile, KEEP, rows, audio_rows)
            for u in range(tiles):
                piece = keep[:, u * BLOCK : (u + 1) * BLOCK]
                for t in range(tiles):
                    seen = blocks[(me ^ a) * tiles + t, (me ^ near) * tiles + u].astype(F32)
                    bias.append(jnp.where(piece * seen > 0.5, 0.0, NEG))
        mine = pl.ds(pl.multiple_of(i * rows, rows), rows)
        spans = [pl.ds(pl.multiple_of((a ^ b) * rows, rows), rows) for b in range(count)]
        for h in range(width // BLOCK):
            lanes = slice(h * BLOCK, (h + 1) * BLOCK)
            parts = [nt(q_all[mine, lanes], k_all[span, lanes]) * scale for span in spans]
            weights, totals = [], []
            for t in range(tiles):
                scores = []
                for b in range(count):
                    for u in range(tiles):
                        piece = parts[b][t * BLOCK : (t + 1) * BLOCK, u * BLOCK : (u + 1) * BLOCK]
                        masked = piece + bias[(b * tiles + u) * tiles + t]
                        if b == 0 and u == t:
                            masked = jnp.where(eye, piece, masked)
                        scores.append(masked)
                scores = join(scores, 1)
                scores = jnp.exp2(scores - jnp.max(scores, axis=1, keepdims=True))
                totals.append(jnp.sum(scores, axis=1, keepdims=True))
                weights.append(scores.astype(BF16))
            weights = join(weights, 0)
            mixed = None
            for b, span in enumerate(spans):
                part = mm(weights[:, b * rows : (b + 1) * rows], v_all[span, lanes])
                mixed = part if mixed is None else mixed + part
            o_all[mine, lanes] = (mixed / join(totals, 0)).astype(BF16)
        return carry

    lax.fori_loop(0, n_q, body, 0)
    for a in range(n_q):
        outs[a][...] = o_all[a * rows : (a + 1) * rows, :]


def video_self_attention(blocks, packs, chosen, rows, audio_rows, own=None):
    count, width = len(packs), packs[0].shape[1]
    extra = [] if own is None else [own]
    n_q = len(chosen)
    keys = count * rows
    scale = BLOCK ** (-0.5) * LOG2E
    return call(
        functools.partial(
            video_self_kernel, count, chosen, own is not None, audio_rows, scale
        ),
        [in_hbm(blocks), *packs, *extra],
        [shape(count * TILE, LANES, dtype=F32)] + [shape(rows, width)] * n_q,
        [pltpu.VMEM((n * rows, width), BF16) for n in (n_q, count, count, n_q)],
        (4 * n_q * rows * keys * width, n_q * rows * keys * width // BLOCK),
        [SMEM] + [VMEM] * (count + len(extra)),
    )


def attend_pair(query, key, value, bias, scale, size):
    lane = lax.broadcasted_iota(jnp.int32, (1, LANES), 1)
    rows, heads = query.shape[0], LANES // size
    masks = [(lane >= i * size) & (lane < (i + 1) * size) for i in range(heads)]
    stacked = join([jnp.where(m, query, jnp.zeros_like(query)) for m in masks], 0)
    parts = nt(stacked, key) * scale
    weights, totals, sums = [], [], []
    for i in range(heads):
        scores = parts[i * rows : (i + 1) * rows] + bias
        top = jnp.max(scores, axis=1, keepdims=True)
        scores = jnp.exp2(scores - top)
        totals.append(jnp.sum(scores, axis=1, keepdims=True))
        sums.append((top, totals[-1]))
        weights.append(scores.astype(BF16))
    mixed = mm(join(weights, 0), value)
    out = mixed[:rows] / totals[0]
    for i in range(1, heads):
        out = jnp.where(masks[i], mixed[i * rows : (i + 1) * rows] / totals[i], out)
    return out, sums


def narrow_job(job, flags, packs, own, outs, k_all, v_all, bias, size, sizes):
    query_flag, key_flag, rows, keys, width, key_at, value_at, query_at, lane = job
    count = len(packs)
    tiles = [flags[j * TILE : (j + 1) * TILE, :] for j in range(count)]
    for j in range(count):
        for held, (row, at) in ((k_all, key_at), (v_all, value_at)):
            held[j * keys : (j + 1) * keys, 0:width] = packs[j][row : row + keys, at : at + width]
    for a, query in enumerate(packs if own is None else [own]):
        if query_flag is not None:
            times = column(flag_row(tiles[a], query_flag, *sizes))
        for b in range(count):
            line = flag_row(tiles[b], key_flag, *sizes)
            if query_flag is not None:
                piece = near_times(times, line)
            else:
                mask = jnp.broadcast_to(line, (rows, keys)) > 0.5
                if a == b:
                    mask = mask | (
                        lax.broadcasted_iota(jnp.int32, (rows, keys), 0)
                        == lax.broadcasted_iota(jnp.int32, (rows, keys), 1)
                    )
                piece = bias_of(mask)
            bias[a * rows : (a + 1) * rows, b * keys : (b + 1) * keys] = piece
        row, at = query_at
        for start in range(0, width, LANES):
            mixed, _ = attend_pair(
                query[row : row + rows, at + start : at + start + LANES],
                k_all[0 : count * keys, start : start + LANES],
                v_all[0 : count * keys, start : start + LANES],
                bias[a * rows : (a + 1) * rows, 0 : count * keys],
                size**-0.5 * LOG2E,
                size,
            )
            outs[a][:, lane + start : lane + start + LANES] = mixed.astype(BF16)


def narrow_kernel(jobs, with_query, count, size, sizes, *refs):
    flags, packs = refs[0], refs[1 : 1 + count]
    own = refs[1 + count] if with_query else None
    outs, held = refs[(2 if with_query else 1) + count : -3], refs[-3:]
    for job in jobs:
        narrow_job(job, flags, packs, own, outs, *held, size, sizes)


def narrow_attention(flags, packs, jobs, sizes, size, own=None):
    count = len(packs)
    extra = [] if own is None else [own]
    n_q = count if own is None else 1
    rows = jobs[0][2]
    keys, width = count * max(job[3] for job in jobs), max(job[4] for job in jobs)
    work = sum(n_q * job[2] * count * job[3] * job[4] for job in jobs)
    return call(
        functools.partial(narrow_kernel, jobs, own is not None, count, size, sizes),
        [flags, *packs, *extra],
        [shape(rows, sum(job[4] for job in jobs))] * n_q,
        [
            pltpu.VMEM((keys, width), BF16),
            pltpu.VMEM((keys, width), BF16),
            pltpu.VMEM((n_q * rows, keys), F32),
        ],
        (8 * work, work // size),
    )


def stat_rows(width, size):
    return -(-3 * (width // size) // TILE) * TILE


def half_kernel(count, size, sizes, *refs):
    flags, packs = refs[0], refs[1 : 1 + count]
    outs, (k_all, v_all) = refs[1 + count : 1 + 2 * count], refs[1 + 2 * count :]
    keys, rows = sizes
    width, near = k_all.shape[1], count // 2
    tiles = [flags[j * TILE : (j + 1) * TILE, :] for j in range(count)]
    for j in range(near):
        k_all[j * keys : (j + 1) * keys, :] = packs[j][0:keys, :]
        v_all[j * keys : (j + 1) * keys, :] = packs[j][keys : 2 * keys, :]
    times = join([flag_row(tiles[j], TIME, *sizes) for j in range(near)], 1)
    lane = lax.broadcasted_iota(jnp.int32, (1, LANES), 1)
    heads, per = width // size, LANES // size
    for a in range(count):
        first = 2 * keys if a < near else 0
        bias = near_times(column(flag_row(tiles[a], AUDIO_TIME, *sizes)), times)
        stats = jnp.zeros((rows, LANES), F32)
        for start in range(0, width, LANES):
            lanes = slice(start, start + LANES)
            mixed, sums = attend_pair(
                packs[a][first : first + rows, lanes],
                k_all[:, lanes],
                v_all[:, lanes],
                bias,
                size**-0.5 * LOG2E,
                size,
            )
            outs[a][0:rows, lanes] = mixed.astype(BF16)
            for i, (top, total) in enumerate(sums):
                rest = top + jnp.log2(total)
                for term in range(3):
                    rounded = rest.astype(BF16).astype(F32)
                    at = term * heads + start // LANES * per + i
                    stats = jnp.where(lane == at, rounded, stats)
                    rest = rest - rounded
        below = outs[a].shape[0] - rows
        outs[a][rows:, 0:rows] = stats.T[0:below, :].astype(BF16)
        if width > rows:
            outs[a][rows:, rows:] = jnp.zeros((below, width - rows), BF16)


def half_attention(flags, packs, sizes, size):
    count, width = len(packs), packs[0].shape[1]
    keys, rows = sizes
    work = count * rows * (count // 2) * keys * width
    return call(
        functools.partial(half_kernel, count, size, sizes),
        [flags, *packs],
        [shape(rows + stat_rows(width, size), width)] * count,
        [pltpu.VMEM((count // 2 * keys, width), BF16)] * 2,
        (8 * work, work // size),
    )


def merge_kernel(count, size, *refs):
    parts, outs = refs[:count], refs[count:]
    rows, width = outs[0].shape
    heads, per = width // size, LANES // size
    lane = lax.broadcasted_iota(jnp.int32, (1, LANES), 1)
    for c, out in enumerate(outs):
        pair = parts[c], parts[c + count // 2]
        sums = []
        for part in pair:
            tile = part[rows:, 0:rows].astype(F32)
            filler = jnp.zeros((LANES - tile.shape[0], rows), F32)
            tile = join([tile, filler], 0).T
            sums.append(
                [
                    tile[:, h : h + 1]
                    + tile[:, heads + h : heads + h + 1]
                    + tile[:, 2 * heads + h : 2 * heads + h + 1]
                    for h in range(heads)
                ]
            )
        for start in range(0, width, LANES):
            lanes = slice(start, start + LANES)
            shares = []
            for i in range(per):
                one, two = (s[start // LANES * per + i] for s in sums)
                top = jnp.maximum(one, two)
                one, two = jnp.exp2(one - top), jnp.exp2(two - top)
                total = one + two
                one, two = one / total, two / total
                if shares:
                    one = jnp.where(lane >= i * size, one, shares[0])
                    two = jnp.where(lane >= i * size, two, shares[1])
                shares = [one, two]
            mixed = shares[0] * pair[0][0:rows, lanes].astype(F32)
            mixed = mixed + shares[1] * pair[1][0:rows, lanes].astype(F32)
            out[:, lanes] = mixed.astype(BF16)


def merge_halves(parts, rows, size):
    count, width = len(parts), parts[0].shape[1]
    return call(
        functools.partial(merge_kernel, count, size),
        parts,
        [shape(rows, width)] * (count // 2),
        [],
        (0, 0),
    )


def project_kernel(places, groups, *refs):
    out, weights, parts = refs[-1], refs[-1 - len(groups) : -1], refs[: -1 - len(groups)]
    me, owner = lax.axis_index("seq"), lax.axis_index("stream")
    _, width = out.shape[1:]
    for i, place in enumerate(places):
        columns = pl.ds(pl.multiple_of((owner ^ place) * width, width), width)
        total = None
        for (indices, lanes), weight in zip(groups, weights):
            for j, index in enumerate(indices):
                at = ((me ^ j) & (len(indices) - 1)) * lanes
                term = mm(parts[index][...], weight[pl.ds(pl.multiple_of(at, lanes), lanes), columns])
                total = term if total is None else total + term
        out[i] = total.astype(out.dtype)


def project(places, groups, weights, rows, columns, dtype):
    parts, layout = [], []
    for members in groups:
        layout.append(([len(parts) + i for i in range(len(members))], members[0].shape[1]))
        parts += members
    depth = sum(w.shape[0] for w in weights)
    return call(
        functools.partial(project_kernel, places, layout),
        [*parts, *weights],
        [shape(len(places), rows, columns, dtype=dtype)],
        [],
        (2 * rows * depth * columns * len(places), 0),
    )[0]


def scatter_sum(terms, count):
    evens = range(0, count, 2)
    arrived = swap(terms([i + 1 for i in evens], BF16), "stream", count, 1)
    kept = terms(list(evens), F32)
    sums = [kept[i] + arrived[i].astype(F32) for i in range(count // 2)]
    distance = 2
    while len(sums) > 1:
        arrived = [swap(s.astype(BF16), "stream", count, distance) for s in sums[1::2]]
        sums = [s + a.astype(F32) for s, a in zip(sums[0::2], arrived)]
        distance *= 2
    return sums[0].astype(BF16)


def shards(
    count,
    streams,
    video_query,
    video_key,
    video_value,
    video_keep,
    video_blocks,
    video_time,
    audio_query,
    audio_key,
    audio_value,
    audio_keep,
    audio_time,
    video_cross_query,
    audio_cross_key,
    audio_cross_value,
    audio_cross_query,
    video_cross_key,
    video_cross_value,
    video_out_w,
    video_cross_w,
    audio_out_w,
    audio_cross_w,
):
    rows, audio_rows = video_query.shape[0], audio_query.shape[0]
    sizes = rows, audio_rows
    size = audio_cross_w.shape[1] // HA
    narrow = audio_query.shape[1]
    flags = (video_keep, video_time, audio_keep, audio_time)
    by_heads = (video_query.shape[1] // BLOCK) % count == 0 and (narrow // LANES) % count == 0
    every, near = range(count), range(count // 2)

    ((heard,),) = pack([(below(audio_cross_key, audio_cross_value), [0], 1)])
    heard = gather_pairs(heard, "seq", count)
    if by_heads:
        (packs,) = pack([(below(video_query, video_key, video_value), every, count)], flags)
        packs = exchange(packs, "seq", count)
        crossed, questions, alone = pack(
            [
                (below(video_cross_key, video_cross_value, audio_cross_query), near, count // 2),
                (below(audio_cross_query), range(count // 2, count), count // 2),
                (below(audio_key, audio_value, audio_query), every, count),
            ],
        )
        crossed = exchange([*crossed, *questions], "seq", count)
        alone = exchange(alone, "seq", count)
    else:
        ((packs,),) = pack([(below(video_key, video_value), [0], 1)], flags)
        packs = gather_pairs(packs, "seq", count)
        (crossed,), (alone,) = pack(
            [
                (below(video_cross_key, video_cross_value), [0], 1),
                (below(audio_key, audio_value), [0], 1),
            ],
        )
        crossed = gather_pairs(crossed, "seq", count)
        alone = gather_pairs(alone, "seq", count)
    staged = pack(
        [(below(w), [0], 1) for w in (video_out_w, video_cross_w, audio_out_w, audio_cross_w)],
    )
    (video_out_w,), (video_cross_w,), (audio_out_w,), (audio_cross_w,) = staged
    if by_heads:
        halves = list(every)[: count // 2], list(every)[count // 2 :]
        all_flags, *far = video_self_attention(video_blocks, packs, halves[1], rows, audio_rows)
        _, *close = video_self_attention(video_blocks, packs, halves[0], rows, audio_rows)
        video_self = exchange([*close, *far], "seq", count)
    else:
        all_flags, *video_self = video_self_attention(
            video_blocks, packs, [0], rows, audio_rows, video_query
        )
    heard_job = (
        *(TIME, AUDIO_TIME, rows, audio_rows, narrow),
        *((0, 0), (audio_rows, 0), (0, 0), 0),
    )
    video_cross = narrow_attention(all_flags, heard, [heard_job], sizes, size, video_cross_query)
    if by_heads:
        audio_cross = half_attention(all_flags, crossed, sizes, size)
        audio_cross = exchange(audio_cross, "seq", count)
        lanes = narrow // count
        self_job = (
            *(None, AUDIO_KEEP, audio_rows, audio_rows, lanes),
            *((0, 0), (audio_rows, 0), (2 * audio_rows, 0), 0),
        )
        audio_self = narrow_attention(all_flags, alone, [self_job], sizes, size)
        audio_self = exchange(audio_self, "seq", count)
        audio_cross = merge_halves(audio_cross, audio_rows, size)
    else:
        cross_job = (
            *(AUDIO_TIME, TIME, audio_rows, rows, narrow),
            *((0, 0), (rows, 0), (0, 0), 0),
        )
        audio_cross = narrow_attention(
            all_flags, crossed, [cross_job], sizes, size, audio_cross_query
        )
        self_job = (
            *(None, AUDIO_KEEP, audio_rows, audio_rows, narrow),
            *((0, 0), (audio_rows, 0), (0, 0), 0),
        )
        audio_self = narrow_attention(all_flags, alone, [self_job], sizes, size, audio_query)

    def terms(groups, weights, rows):
        columns = weights[0].shape[1] // streams
        return lambda places, dtype: project(places, groups, weights, rows, columns, dtype)

    video_update = scatter_sum(
        terms([video_self, video_cross], [video_out_w, video_cross_w], rows), streams
    )
    audio_update = scatter_sum(
        terms([audio_self, audio_cross], [audio_out_w, audio_cross_w], audio_rows), streams
    )
    return video_update, audio_update


def solution(mesh):
    tokens = P(("dp", "seq"))
    matrix = P(("dp", "seq"), "stream")
    weight = P("stream", None)
    count, streams = mesh.shape["seq"], mesh.shape["stream"]

    def body(*args):
        return shards(count, streams, *args)

    return jax.shard_map(
        body,
        mesh=mesh,
        in_specs=(
            matrix,
            matrix,
            matrix,
            tokens,
            P("dp", None),
            tokens,
            matrix,
            matrix,
            matrix,
            tokens,
            tokens,
            matrix,
            matrix,
            matrix,
            matrix,
            matrix,
            matrix,
            weight,
            weight,
            weight,
            weight,
        ),
        out_specs=(matrix, matrix),
        check_vma=False,
    )
```

```python
import functools
import math

import jax
import jax.numpy as jnp
from jax import lax
from jax.experimental import pallas as pl
from jax.experimental.pallas import tpu as pltpu
from jax.sharding import PartitionSpec as P

HA = 32
BLOCK = 128
WINDOW = 10
LANES = 128
TILE = 16
NEG = -1e30
LOG2E = math.log2(math.e)
F32 = jnp.float32
BF16 = jnp.bfloat16
VMEM = pl.BlockSpec(memory_space=pltpu.VMEM)
SMEM = pl.BlockSpec(memory_space=pltpu.SMEM)
HBM = pl.BlockSpec(memory_space=pltpu.HBM)
MIB = 1 << 20
SEQ, STREAM, DP = "seq", "stream", "dp"


def swap(x, axis, count, distance):
    return lax.ppermute(x, axis, [(i, i ^ distance) for i in range(count)])


def far_first(count):
    return [*range(count // 2, count), *range(1, count // 2)]


def exchange(pieces, axis, count):
    arrived = {j: swap(pieces[j], axis, count, j) for j in far_first(count)}
    return [pieces[0]] + [arrived[j] for j in range(1, count)]


def gather_pairs(x, axis, count):
    blocks = {0: x}
    distance = count // 2
    while distance:
        for j in sorted(blocks):
            blocks[j ^ distance] = swap(blocks[j], axis, count, distance)
        distance //= 2
    return [blocks[j] for j in range(count)]


def call(kernel, operands, outs, scratch, work, specs=None, sems=()):
    blocked = [a for a, spec in zip(operands, specs or [VMEM] * len(operands)) if spec is not HBM]
    size = sum(a.size * a.dtype.itemsize for a in [*blocked, *outs])
    held = sum(math.prod(s.shape) * jnp.dtype(s.dtype).itemsize for s in scratch)
    flops, exps = work
    return pl.pallas_call(
        kernel,
        out_shape=outs,
        in_specs=specs or [VMEM] * len(operands),
        out_specs=[VMEM] * len(outs),
        scratch_shapes=[*scratch, *sems],
        compiler_params=pltpu.CompilerParams(vmem_limit_bytes=size + held + 8 * MIB),
        cost_estimate=pl.CostEstimate(
            flops=int(flops), bytes_accessed=int(size), transcendentals=int(exps)
        ),
    )(*operands)


def shape(*dims, dtype=BF16):
    return jax.ShapeDtypeStruct(dims, dtype)


def nt(a, b):
    return lax.dot_general(a, b, (((1,), (1,)), ((), ())), preferred_element_type=F32)


def mm(a, b):
    return jnp.dot(a, b, preferred_element_type=F32)


def join(parts, axis):
    return parts[0] if len(parts) == 1 else jnp.concatenate(parts, axis=axis)


def square_eye():
    return lax.broadcasted_iota(jnp.int32, (LANES, LANES), 0) == lax.broadcasted_iota(
        jnp.int32, (LANES, LANES), 1
    )


def column(row):
    eye, parts = square_eye(), []
    for start in range(0, row.shape[1], LANES):
        piece = row[:, start : start + LANES]
        parts.append(jnp.sum(jnp.where(eye, piece, 0.0), axis=1, keepdims=True))
    return join(parts, 0)


def bias_of(allowed):
    return jnp.where(allowed, 0.0, NEG)


def near_times(query_column, key_row):
    return bias_of(jnp.abs(query_column - key_row) <= WINDOW)


def flag_kernel(*refs):
    flags, out, held, sems = refs[:4], refs[4], refs[5:9], refs[9]
    copies = [pltpu.make_async_copy(f, h, sems.at[i]) for i, (f, h) in enumerate(zip(flags, held))]
    for copy in copies:
        copy.start()
    for copy in copies:
        copy.wait()
    index = lax.broadcasted_iota(jnp.int32, (TILE, LANES), 0)
    tile = jnp.zeros((TILE, LANES), F32)
    at = 0
    for flag in held:
        values = flag[...].astype(F32)
        for start in range(0, values.shape[1], LANES):
            tile = jnp.where(index == at, values[:, start : start + LANES], tile)
            at += 1
    out[...] = tile.astype(BF16)


def flag_tile(*flags):
    return call(
        flag_kernel,
        [in_hbm(f.reshape(1, -1)) for f in flags],
        [shape(TILE, LANES)],
        [pltpu.VMEM((1, f.shape[0]), jnp.int32) for f in flags],
        (0, 0),
        [HBM] * 4,
        [pltpu.SemaphoreType.DMA((4,))],
    )[0]


def flag_row(tile, which, rows, audio_rows):
    counts = [rows // LANES, rows // LANES, audio_rows // LANES, audio_rows // LANES]
    at = sum(counts[:which])
    return join([tile[i : i + 1, :] for i in range(at, at + counts[which])], 1)


KEEP, TIME, AUDIO_KEEP, AUDIO_TIME = range(4)


def pack_kernel(groups, *refs):
    n_in = sum(len(layout) for layout, _, _ in groups)
    inputs, outs, sems = refs[:n_in], refs[n_in:-1], refs[-1]
    me = lax.axis_index(SEQ)
    copies = []
    first_in = first_out = 0
    for layout, places, parts in groups:
        for out, j in zip(outs[first_out:], places):
            for array, (row, lane) in zip(inputs[first_in:], layout):
                rows, width = array.shape[0], array.shape[1] // parts
                columns = slice(None)
                if parts > 1:
                    part = (me ^ j) & (parts - 1)
                    columns = pl.ds(pl.multiple_of(part * width, width), width)
                target = out.at[row : row + rows, lane : lane + width]
                copies.append(
                    pltpu.make_async_copy(array.at[:, columns], target, sems.at[len(copies)])
                )
        first_in, first_out = first_in + len(layout), first_out + len(places)
    for copy in copies:
        copy.start()
    for copy in copies:
        copy.wait()


def in_hbm(array):
    return pltpu.with_memory_space_constraint(array, pltpu.HBM)


def pack(groups):
    outs, layout, arrays = [], [], []
    for placed, places, parts in groups:
        rows = max(row + a.shape[0] for a, row, _ in placed)
        width = max(lane + a.shape[1] // parts for a, _, lane in placed)
        outs += [shape(rows, width, dtype=placed[0][0].dtype)] * len(places)
        layout.append(([(row, lane) for _, row, lane in placed], list(places), parts))
        arrays += [a for a, _, _ in placed]
    copies = sum(len(spots) * len(places) for spots, places, _ in layout)
    got = call(
        functools.partial(pack_kernel, layout),
        [in_hbm(a) for a in arrays],
        outs,
        [],
        (0, 0),
        [HBM] * len(arrays),
        [pltpu.SemaphoreType.DMA((copies,))],
    )
    split_up, at = [], 0
    for _, places, _ in groups:
        split_up.append(got[at : at + len(places)])
        at += len(places)
    return split_up


def below(*arrays):
    placed, row = [], 0
    for array in arrays:
        placed.append((array, row, 0))
        row += array.shape[0]
    return placed


def video_self_kernel(count, chosen, with_query, audio_rows, scale, *refs):
    blocks, flags, packs = refs[0], refs[1 : 1 + count], refs[1 + count : 1 + 2 * count]
    queries = [refs[1 + 2 * count]] if with_query else [packs[a] for a in chosen]
    outs = refs[-len(chosen) :]
    rows, width = outs[0].shape
    tiles = rows // BLOCK
    me = lax.axis_index(SEQ)
    at = 0 if with_query else rows
    keys = [pack.at[at : at + rows, :] for pack in packs]
    values = [pack.at[at + rows : at + 2 * rows, :] for pack in packs]
    kept = [flag_row(f[...].astype(F32), KEEP, rows, audio_rows) for f in flags]
    eye = square_eye()
    for a, query, out in zip(chosen, queries, outs):
        bias = {}
        for b in range(count):
            for u in range(tiles):
                piece = kept[b][:, u * BLOCK : (u + 1) * BLOCK]
                for t in range(tiles):
                    seen = blocks[(me ^ a) * tiles + t, (me ^ b) * tiles + u].astype(F32)
                    bias[b, u, t] = jnp.where(piece * seen > 0.5, 0.0, NEG)
        for h in range(width // BLOCK):
            lanes = slice(h * BLOCK, (h + 1) * BLOCK)
            parts = [nt(query[0:rows, lanes], key[:, lanes]) * scale for key in keys]
            weights, totals = [], []
            for t in range(tiles):
                scores = []
                for b in range(count):
                    for u in range(tiles):
                        piece = parts[b][t * BLOCK : (t + 1) * BLOCK, u * BLOCK : (u + 1) * BLOCK]
                        masked = piece + bias[b, u, t]
                        if a == b and u == t:
                            masked = jnp.where(eye, piece, masked)
                        scores.append(masked)
                scores = join(scores, 1)
                scores = jnp.exp2(scores - jnp.max(scores, axis=1, keepdims=True))
                totals.append(jnp.sum(scores, axis=1, keepdims=True))
                weights.append(scores.astype(BF16))
            weights = join(weights, 0)
            mixed = None
            for b, value in enumerate(values):
                part = mm(weights[:, b * rows : (b + 1) * rows], value[:, lanes])
                mixed = part if mixed is None else mixed + part
            out[:, lanes] = (mixed / join(totals, 0)).astype(BF16)


def video_self_attention(blocks, flags, packs, chosen, rows, audio_rows, own=None):
    count, width = len(packs), packs[0].shape[1]
    extra = [] if own is None else [own]
    n_q = len(chosen)
    keys = count * rows
    scale = BLOCK ** (-0.5) * LOG2E
    return call(
        functools.partial(
            video_self_kernel, count, chosen, own is not None, audio_rows, scale
        ),
        [in_hbm(blocks), *flags, *packs, *extra],
        [shape(rows, width)] * n_q,
        [],
        (4 * n_q * rows * keys * width, n_q * rows * keys * width // BLOCK),
        [SMEM] + [VMEM] * (2 * count + len(extra)),
    )


def attend_pair(query, key, value, bias, scale, size):
    lane = lax.broadcasted_iota(jnp.int32, (1, LANES), 1)
    rows, heads = query.shape[0], LANES // size
    masks = [(lane >= i * size) & (lane < (i + 1) * size) for i in range(heads)]
    stacked = join([jnp.where(m, query, jnp.zeros_like(query)) for m in masks], 0)
    parts = nt(stacked, key) * scale
    weights, totals, sums = [], [], []
    for i in range(heads):
        scores = parts[i * rows : (i + 1) * rows] + bias
        top = jnp.max(scores, axis=1, keepdims=True)
        scores = jnp.exp2(scores - top)
        totals.append(jnp.sum(scores, axis=1, keepdims=True))
        sums.append((top, totals[-1]))
        weights.append(scores.astype(BF16))
    mixed = mm(join(weights, 0), value)
    out = mixed[:rows] / totals[0]
    for i in range(1, heads):
        out = jnp.where(masks[i], mixed[i * rows : (i + 1) * rows] / totals[i], out)
    return out, sums


def narrow_kernel(job, layout, size, sizes, *refs):
    query_flag, key_flag, rows, keys, key_row, value_row, query_row = job
    key_refs, value_refs, query_refs = ([refs[i] for i in part] for part in layout)
    count = len(key_refs)
    tiles = [f[...].astype(F32) for f in refs[:count]]
    outs, (k_all, v_all, bias) = refs[-3 - len(query_refs) : -3], refs[-3:]
    for held, group, row in ((k_all, key_refs, key_row), (v_all, value_refs, value_row)):
        for j, ref in enumerate(group):
            held[j * keys : (j + 1) * keys, :] = ref[row : row + keys, :]
    for a, query in enumerate(query_refs):
        if query_flag is not None:
            times = column(flag_row(tiles[a], query_flag, *sizes))
        for b in range(count):
            line = flag_row(tiles[b], key_flag, *sizes)
            if query_flag is not None:
                piece = near_times(times, line)
            else:
                mask = jnp.broadcast_to(line, (rows, keys)) > 0.5
                if a == b:
                    mask = mask | (
                        lax.broadcasted_iota(jnp.int32, (rows, keys), 0)
                        == lax.broadcasted_iota(jnp.int32, (rows, keys), 1)
                    )
                piece = bias_of(mask)
            bias[:, b * keys : (b + 1) * keys] = piece
        for start in range(0, k_all.shape[1], LANES):
            lanes = slice(start, start + LANES)
            mixed, _ = attend_pair(
                query[query_row : query_row + rows, lanes],
                k_all[:, lanes],
                v_all[:, lanes],
                bias[...],
                size**-0.5 * LOG2E,
                size,
            )
            outs[a][:, lanes] = mixed.astype(BF16)


def narrow_attention(flags, keys, values, queries, job, sizes, size):
    operands, layout = list(flags), []
    for group in (keys, values, queries):
        indices = []
        for array in group:
            known = [i for i, operand in enumerate(operands) if operand is array]
            indices.append(known[0] if known else len(operands))
            if not known:
                operands.append(array)
        layout.append(indices)
    rows, all_keys, width = job[2], len(keys) * job[3], keys[0].shape[1]
    work = len(queries) * rows * all_keys * width
    return call(
        functools.partial(narrow_kernel, job, layout, size, sizes),
        operands,
        [shape(rows, width)] * len(queries),
        [
            pltpu.VMEM((all_keys, width), BF16),
            pltpu.VMEM((all_keys, width), BF16),
            pltpu.VMEM((rows, all_keys), F32),
        ],
        (8 * work, work // size),
    )


def stat_rows(width, size):
    return -(-3 * (width // size) // TILE) * TILE


def half_kernel(count, size, sizes, *refs):
    tiles, packs = [f[...].astype(F32) for f in refs[:count]], refs[count : 2 * count]
    outs, (k_all, v_all) = refs[2 * count : 3 * count], refs[3 * count :]
    keys, rows = sizes
    width, near = k_all.shape[1], count // 2
    for j in range(near):
        k_all[j * keys : (j + 1) * keys, :] = packs[j][0:keys, :]
        v_all[j * keys : (j + 1) * keys, :] = packs[j][keys : 2 * keys, :]
    times = join([flag_row(tiles[j], TIME, *sizes) for j in range(near)], 1)
    lane = lax.broadcasted_iota(jnp.int32, (1, LANES), 1)
    heads, per = width // size, LANES // size
    for a in range(count):
        first = 2 * keys if a < near else 0
        bias = near_times(column(flag_row(tiles[a], AUDIO_TIME, *sizes)), times)
        stats = jnp.zeros((rows, LANES), F32)
        for start in range(0, width, LANES):
            lanes = slice(start, start + LANES)
            mixed, sums = attend_pair(
                packs[a][first : first + rows, lanes],
                k_all[:, lanes],
                v_all[:, lanes],
                bias,
                size**-0.5 * LOG2E,
                size,
            )
            outs[a][0:rows, lanes] = mixed.astype(BF16)
            for i, (top, total) in enumerate(sums):
                rest = top + jnp.log2(total)
                for term in range(3):
                    rounded = rest.astype(BF16).astype(F32)
                    at = term * heads + start // LANES * per + i
                    stats = jnp.where(lane == at, rounded, stats)
                    rest = rest - rounded
        below = outs[a].shape[0] - rows
        outs[a][rows:, 0:rows] = stats.T[0:below, :].astype(BF16)
        if width > rows:
            outs[a][rows:, rows:] = jnp.zeros((below, width - rows), BF16)


def half_attention(flags, packs, sizes, size):
    count, width = len(packs), packs[0].shape[1]
    keys, rows = sizes
    work = count * rows * (count // 2) * keys * width
    return call(
        functools.partial(half_kernel, count, size, sizes),
        [*flags, *packs],
        [shape(rows + stat_rows(width, size), width)] * count,
        [pltpu.VMEM((count // 2 * keys, width), BF16)] * 2,
        (8 * work, work // size),
    )


def merge_kernel(count, size, *refs):
    parts, outs = refs[:count], refs[count:]
    rows, width = outs[0].shape
    heads, per = width // size, LANES // size
    lane = lax.broadcasted_iota(jnp.int32, (1, LANES), 1)
    for c, out in enumerate(outs):
        pair = parts[c], parts[c + count // 2]
        sums = []
        for part in pair:
            tile = part[rows:, 0:rows].astype(F32)
            filler = jnp.zeros((LANES - tile.shape[0], rows), F32)
            tile = join([tile, filler], 0).T
            sums.append(
                [
                    tile[:, h : h + 1]
                    + tile[:, heads + h : heads + h + 1]
                    + tile[:, 2 * heads + h : 2 * heads + h + 1]
                    for h in range(heads)
                ]
            )
        for start in range(0, width, LANES):
            lanes = slice(start, start + LANES)
            shares = []
            for i in range(per):
                one, two = (s[start // LANES * per + i] for s in sums)
                top = jnp.maximum(one, two)
                one, two = jnp.exp2(one - top), jnp.exp2(two - top)
                total = one + two
                one, two = one / total, two / total
                if shares:
                    one = jnp.where(lane >= i * size, one, shares[0])
                    two = jnp.where(lane >= i * size, two, shares[1])
                shares = [one, two]
            mixed = shares[0] * pair[0][0:rows, lanes].astype(F32)
            mixed = mixed + shares[1] * pair[1][0:rows, lanes].astype(F32)
            out[:, lanes] = mixed.astype(BF16)


def merge_halves(parts, rows, size):
    count, width = len(parts), parts[0].shape[1]
    return call(
        functools.partial(merge_kernel, count, size),
        parts,
        [shape(rows, width)] * (count // 2),
        [],
        (0, 0),
    )


def project_kernel(places, groups, with_before, *refs):
    out, refs = refs[-1], refs[:-1]
    before, refs = (refs[-1], refs[:-1]) if with_before else (None, refs)
    weights, parts = refs[len(refs) - len(groups) :], refs[: len(refs) - len(groups)]
    me, owner = lax.axis_index(SEQ), lax.axis_index(STREAM)
    _, width = out.shape[1:]
    for i, place in enumerate(places):
        columns = pl.ds(pl.multiple_of((owner ^ place) * width, width), width)
        total = before[place] if with_before else None
        for (indices, lanes), weight in zip(groups, weights):
            for j, index in enumerate(indices):
                at = ((me ^ j) & (len(indices) - 1)) * lanes
                term = mm(parts[index][...], weight[pl.ds(pl.multiple_of(at, lanes), lanes), columns])
                total = term if total is None else total + term
        out[i] = total.astype(out.dtype)


def project(places, groups, weights, rows, columns, dtype, before=None):
    parts, layout = [], []
    for members in groups:
        layout.append(([len(parts) + i for i in range(len(members))], members[0].shape[1]))
        parts += members
    depth = sum(w.shape[0] for w in weights)
    return call(
        functools.partial(project_kernel, places, layout, before is not None),
        [*parts, *weights, *([] if before is None else [before])],
        [shape(len(places), rows, columns, dtype=dtype)],
        [],
        (2 * rows * depth * columns * len(places), 0),
    )[0]


def collect_kernel(layout, *refs):
    out = refs[-1]
    for k, entries in enumerate(layout):
        total = functools.reduce(jnp.add, [refs[i][at].astype(F32) for i, at in entries])
        if len(out.shape) == 2:
            out[...] = total.astype(BF16)
        else:
            out[k] = total.astype(BF16)


def collect(sums, final=False):
    operands, layout = [], []
    for terms in sums:
        entries = []
        for array, at in terms:
            known = [i for i, operand in enumerate(operands) if operand is array]
            entries.append((known[0] if known else len(operands), at))
            if not known:
                operands.append(array)
        layout.append(entries)
    block = operands[0].shape[1:]
    out = shape(*block) if final else shape(len(sums), *block)
    return call(functools.partial(collect_kernel, layout), operands, [out], [], (0, 0))[0]


def scatter_sum(terms, count, one_by_one):
    half = count // 2
    if one_by_one:
        parts = {}
        for i in reversed(range(half)):
            arrived = swap(terms([2 * i + 1], BF16), STREAM, count, 1)
            parts[i] = [(terms([2 * i], F32), 0), (arrived, 0)]
    else:
        arrived = swap(terms(list(range(1, count, 2)), BF16), STREAM, count, 1)
        kept = terms(list(range(0, count, 2)), F32)
        parts = {i: [(kept, i), (arrived, i)] for i in range(half)}
    distance = 2
    while distance < count:
        leaving = [i for i in sorted(parts) if 2 * i & distance]
        sent = collect([parts.pop(i) for i in leaving])
        arrived = swap(sent, STREAM, count, distance)
        for k, i in enumerate(sorted(parts)):
            parts[i].append((arrived, k))
        distance *= 2
    return collect([parts[0]], True)


def shards(
    count,
    streams,
    video_query,
    video_key,
    video_value,
    video_keep,
    video_blocks,
    video_time,
    audio_query,
    audio_key,
    audio_value,
    audio_keep,
    audio_time,
    video_cross_query,
    audio_cross_key,
    audio_cross_value,
    audio_cross_query,
    video_cross_key,
    video_cross_value,
    video_out_w,
    video_cross_w,
    audio_out_w,
    audio_cross_w,
):
    rows, audio_rows = video_query.shape[0], audio_query.shape[0]
    sizes = rows, audio_rows
    size = audio_cross_w.shape[1] // HA
    narrow = audio_query.shape[1]
    by_heads = (video_query.shape[1] // BLOCK) % count == 0 and (narrow // LANES) % count == 0
    every, near = range(count), range(count // 2)

    heard_keys = gather_pairs(audio_cross_key, SEQ, count)
    heard_values = gather_pairs(audio_cross_value, SEQ, count)
    flags = flag_tile(video_keep, video_time, audio_keep, audio_time)
    if by_heads:
        (packs,) = pack([(below(video_query, video_key, video_value), every, count)])
        packs = exchange(packs, SEQ, count)
        flags = exchange([flags] * count, SEQ, count)
        crossed, questions, alone = pack(
            [
                (below(video_cross_key, video_cross_value, audio_cross_query), near, count // 2),
                (below(audio_cross_query), range(count // 2, count), count // 2),
                (below(audio_key, audio_value, audio_query), every, count),
            ],
        )
        crossed = exchange([*crossed, *questions], SEQ, count)
        alone = exchange(alone, SEQ, count)
    else:
        ((packs,),) = pack([(below(video_key, video_value), [0], 1)])
        packs = gather_pairs(packs, SEQ, count)
        flags = gather_pairs(flags, SEQ, count)
        (crossed,), (alone,) = pack(
            [
                (below(video_cross_key, video_cross_value), [0], 1),
                (below(audio_key, audio_value), [0], 1),
            ],
        )
        crossed = gather_pairs(crossed, SEQ, count)
        alone = gather_pairs(alone, SEQ, count)
    staged = pack(
        [(below(w), [0], 1) for w in (video_out_w, video_cross_w, audio_out_w, audio_cross_w)],
    )
    (video_out_w,), (video_cross_w,), (audio_out_w,), (audio_cross_w,) = staged

    def video_attention(chosen, own=None):
        return video_self_attention(video_blocks, flags, packs, chosen, rows, audio_rows, own)

    if by_heads:
        far = video_attention(list(every)[count // 2 :])
        close = video_attention(list(near))
        video_self = exchange([*close, *far], SEQ, count)
    else:
        video_self = video_attention([0], video_query)

    def audio_attention(keys, values, queries, *job):
        return narrow_attention(flags, keys, values, queries, job, sizes, size)

    video_cross = audio_attention(
        heard_keys,
        heard_values,
        [video_cross_query],
        *(TIME, AUDIO_TIME, rows, audio_rows, 0, 0, 0),
    )
    if by_heads:
        audio_cross = half_attention(flags, crossed, sizes, size)
        audio_cross = exchange(audio_cross, SEQ, count)
        audio_self = audio_attention(
            *(alone, alone, alone),
            *(None, AUDIO_KEEP, audio_rows, audio_rows, 0, audio_rows, 2 * audio_rows),
        )
        audio_self = exchange(audio_self, SEQ, count)
        audio_cross = merge_halves(audio_cross, audio_rows, size)
    else:
        audio_cross = audio_attention(
            *(crossed, crossed, [audio_cross_query]),
            *(AUDIO_TIME, TIME, audio_rows, rows, 0, rows, 0),
        )
        audio_self = audio_attention(
            *(alone, alone, [audio_query]),
            *(None, AUDIO_KEEP, audio_rows, audio_rows, 0, audio_rows, 0),
        )

    def terms(groups, weights, rows, before=None):
        columns = weights[0].shape[1] // streams
        return lambda places, dtype: project(places, groups, weights, rows, columns, dtype, before)

    video_update = scatter_sum(
        terms([video_self, video_cross], [video_out_w, video_cross_w], rows), streams, True
    )
    early = terms([audio_cross], [audio_cross_w], audio_rows)
    early = early(list(range(streams)), F32)
    audio_update = scatter_sum(terms([audio_self], [audio_out_w], audio_rows, early), streams, True)
    return video_update, audio_update


def solution(mesh):
    tokens = P((DP, SEQ))
    matrix = P((DP, SEQ), STREAM)
    weight = P(STREAM, None)
    count, streams = mesh.shape[SEQ], mesh.shape[STREAM]

    def body(*args):
        return shards(count, streams, *args)

    return jax.shard_map(
        body,
        mesh=mesh,
        in_specs=(
            matrix,
            matrix,
            matrix,
            tokens,
            P(DP, None),
            tokens,
            matrix,
            matrix,
            matrix,
            tokens,
            tokens,
            matrix,
            matrix,
            matrix,
            matrix,
            matrix,
            matrix,
            weight,
            weight,
            weight,
            weight,
        ),
        out_specs=(matrix, matrix),
        check_vma=False,
    )
```

```python
import functools
import math

import jax
import jax.numpy as jnp
from jax import lax
from jax.experimental import pallas as pl
from jax.experimental.pallas import tpu as pltpu
from jax.sharding import PartitionSpec as P

HA = 32
BLOCK = 128
WINDOW = 10
LANES = 128
TILE = 16
NEG = -1e30
LOG2E = math.log2(math.e)
F32 = jnp.float32
BF16 = jnp.bfloat16
VMEM = pl.BlockSpec(memory_space=pltpu.VMEM)
SMEM = pl.BlockSpec(memory_space=pltpu.SMEM)
HBM = pl.BlockSpec(memory_space=pltpu.HBM)
MIB = 1 << 20
SEQ, STREAM, DP = "seq", "stream", "dp"


def swap(x, axis, count, distance):
    return lax.ppermute(x, axis, [(i, i ^ distance) for i in range(count)])


def far_first(count):
    return [*range(count // 2, count), *range(1, count // 2)]


def exchange(pieces, axis, count):
    arrived = {j: swap(pieces[j], axis, count, j) for j in far_first(count)}
    return [pieces[0]] + [arrived[j] for j in range(1, count)]


def gather_pairs(x, axis, count):
    blocks = {0: x}
    distance = count // 2
    while distance:
        for j in sorted(blocks):
            blocks[j ^ distance] = swap(blocks[j], axis, count, distance)
        distance //= 2
    return [blocks[j] for j in range(count)]


def call(kernel, operands, outs, scratch, work, specs=None, sems=()):
    blocked = [a for a, spec in zip(operands, specs or [VMEM] * len(operands)) if spec is not HBM]
    size = sum(a.size * a.dtype.itemsize for a in [*blocked, *outs])
    held = sum(math.prod(s.shape) * jnp.dtype(s.dtype).itemsize for s in scratch)
    flops, exps = work
    return pl.pallas_call(
        kernel,
        out_shape=outs,
        in_specs=specs or [VMEM] * len(operands),
        out_specs=[VMEM] * len(outs),
        scratch_shapes=[*scratch, *sems],
        compiler_params=pltpu.CompilerParams(vmem_limit_bytes=size + held + 8 * MIB),
        cost_estimate=pl.CostEstimate(
            flops=int(flops), bytes_accessed=int(size), transcendentals=int(exps)
        ),
    )(*operands)


def shape(*dims, dtype=BF16):
    return jax.ShapeDtypeStruct(dims, dtype)


def nt(a, b):
    return lax.dot_general(a, b, (((1,), (1,)), ((), ())), preferred_element_type=F32)


def mm(a, b):
    return jnp.dot(a, b, preferred_element_type=F32)


def join(parts, axis):
    return parts[0] if len(parts) == 1 else jnp.concatenate(parts, axis=axis)


def square_eye():
    return lax.broadcasted_iota(jnp.int32, (LANES, LANES), 0) == lax.broadcasted_iota(
        jnp.int32, (LANES, LANES), 1
    )


def column(row):
    eye, parts = square_eye(), []
    for start in range(0, row.shape[1], LANES):
        piece = row[:, start : start + LANES]
        parts.append(jnp.sum(jnp.where(eye, piece, 0.0), axis=1, keepdims=True))
    return join(parts, 0)


def bias_of(allowed):
    return jnp.where(allowed, 0.0, NEG)


def near_times(query_column, key_row):
    return bias_of(jnp.abs(query_column - key_row) <= WINDOW)


def flag_kernel(*refs):
    flags, out, held, sems = refs[:4], refs[4], refs[5:9], refs[9]
    copies = [pltpu.make_async_copy(f, h, sems.at[i]) for i, (f, h) in enumerate(zip(flags, held))]
    for copy in copies:
        copy.start()
    for copy in copies:
        copy.wait()
    index = lax.broadcasted_iota(jnp.int32, (TILE, LANES), 0)
    tile = jnp.zeros((TILE, LANES), F32)
    at = 0
    for flag in held:
        values = flag[...].astype(F32)
        for start in range(0, values.shape[1], LANES):
            tile = jnp.where(index == at, values[:, start : start + LANES], tile)
            at += 1
    out[...] = tile.astype(BF16)


def flag_tile(*flags):
    return call(
        flag_kernel,
        [in_hbm(f.reshape(1, -1)) for f in flags],
        [shape(TILE, LANES)],
        [pltpu.VMEM((1, f.shape[0]), jnp.int32) for f in flags],
        (0, 0),
        [HBM] * 4,
        [pltpu.SemaphoreType.DMA((4,))],
    )[0]


def flag_row(tile, which, rows, audio_rows):
    counts = [rows // LANES, rows // LANES, audio_rows // LANES, audio_rows // LANES]
    at = sum(counts[:which])
    return join([tile[i : i + 1, :] for i in range(at, at + counts[which])], 1)


KEEP, TIME, AUDIO_KEEP, AUDIO_TIME = range(4)


def pack_kernel(groups, *refs):
    n_in = sum(len(layout) for layout, _, _ in groups)
    inputs, outs, sems = refs[:n_in], refs[n_in:-1], refs[-1]
    me = lax.axis_index(SEQ)
    copies = []
    first_in = first_out = 0
    for layout, places, parts in groups:
        for out, j in zip(outs[first_out:], places):
            for array, (row, lane) in zip(inputs[first_in:], layout):
                rows, width = array.shape[0], array.shape[1] // parts
                columns = slice(None)
                if parts > 1:
                    part = (me ^ j) & (parts - 1)
                    columns = pl.ds(pl.multiple_of(part * width, width), width)
                target = out.at[row : row + rows, lane : lane + width]
                copies.append(
                    pltpu.make_async_copy(array.at[:, columns], target, sems.at[len(copies)])
                )
        first_in, first_out = first_in + len(layout), first_out + len(places)
    for copy in copies:
        copy.start()
    for copy in copies:
        copy.wait()


def in_hbm(array):
    return pltpu.with_memory_space_constraint(array, pltpu.HBM)


def pack(groups):
    outs, layout, arrays = [], [], []
    for placed, places, parts in groups:
        rows = max(row + a.shape[0] for a, row, _ in placed)
        width = max(lane + a.shape[1] // parts for a, _, lane in placed)
        outs += [shape(rows, width, dtype=placed[0][0].dtype)] * len(places)
        layout.append(([(row, lane) for _, row, lane in placed], list(places), parts))
        arrays += [a for a, _, _ in placed]
    copies = sum(len(spots) * len(places) for spots, places, _ in layout)
    got = call(
        functools.partial(pack_kernel, layout),
        [in_hbm(a) for a in arrays],
        outs,
        [],
        (0, 0),
        [HBM] * len(arrays),
        [pltpu.SemaphoreType.DMA((copies,))],
    )
    split_up, at = [], 0
    for _, places, _ in groups:
        split_up.append(got[at : at + len(places)])
        at += len(places)
    return split_up


def below(*arrays):
    placed, row = [], 0
    for array in arrays:
        placed.append((array, row, 0))
        row += array.shape[0]
    return placed


def video_self_kernel(count, chosen, with_query, audio_rows, scale, *refs):
    blocks, flags, packs = refs[0], refs[1 : 1 + count], refs[1 + count : 1 + 2 * count]
    queries = [refs[1 + 2 * count]] if with_query else [packs[a] for a in chosen]
    outs = refs[-len(chosen) :]
    rows, width = outs[0].shape
    tiles = rows // BLOCK
    me = lax.axis_index(SEQ)
    at = 0 if with_query else rows
    keys = [pack.at[at : at + rows, :] for pack in packs]
    values = [pack.at[at + rows : at + 2 * rows, :] for pack in packs]
    kept = [flag_row(f[...].astype(F32), KEEP, rows, audio_rows) for f in flags]
    eye = square_eye()
    for a, query, out in zip(chosen, queries, outs):
        bias = {}
        for b in range(count):
            for u in range(tiles):
                piece = kept[b][:, u * BLOCK : (u + 1) * BLOCK]
                for t in range(tiles):
                    seen = blocks[(me ^ a) * tiles + t, (me ^ b) * tiles + u].astype(F32)
                    bias[b, u, t] = jnp.where(piece * seen > 0.5, 0.0, NEG)
        for h in range(width // BLOCK):
            lanes = slice(h * BLOCK, (h + 1) * BLOCK)
            parts = [nt(query[0:rows, lanes], key[:, lanes]) * scale for key in keys]
            weights, totals = [], []
            for t in range(tiles):
                scores = []
                for b in range(count):
                    for u in range(tiles):
                        piece = parts[b][t * BLOCK : (t + 1) * BLOCK, u * BLOCK : (u + 1) * BLOCK]
                        masked = piece + bias[b, u, t]
                        if a == b and u == t:
                            masked = jnp.where(eye, piece, masked)
                        scores.append(masked)
                scores = join(scores, 1)
                scores = jnp.exp2(scores - jnp.max(scores, axis=1, keepdims=True))
                totals.append(jnp.sum(scores, axis=1, keepdims=True))
                weights.append(scores.astype(BF16))
            weights = join(weights, 0)
            mixed = None
            for b, value in enumerate(values):
                part = mm(weights[:, b * rows : (b + 1) * rows], value[:, lanes])
                mixed = part if mixed is None else mixed + part
            out[:, lanes] = (mixed / join(totals, 0)).astype(BF16)


def video_self_attention(blocks, flags, packs, chosen, rows, audio_rows, own=None):
    count, width = len(packs), packs[0].shape[1]
    extra = [] if own is None else [own]
    n_q = len(chosen)
    keys = count * rows
    scale = BLOCK ** (-0.5) * LOG2E
    return call(
        functools.partial(
            video_self_kernel, count, chosen, own is not None, audio_rows, scale
        ),
        [in_hbm(blocks), *flags, *packs, *extra],
        [shape(rows, width)] * n_q,
        [],
        (4 * n_q * rows * keys * width, n_q * rows * keys * width // BLOCK),
        [SMEM] + [VMEM] * (2 * count + len(extra)),
    )


def attend_pair(query, key, value, bias, scale, size):
    lane = lax.broadcasted_iota(jnp.int32, (1, LANES), 1)
    rows, heads = query.shape[0], LANES // size
    masks = [(lane >= i * size) & (lane < (i + 1) * size) for i in range(heads)]
    stacked = join([jnp.where(m, query, jnp.zeros_like(query)) for m in masks], 0)
    parts = nt(stacked, key) * scale
    weights, totals, sums = [], [], []
    for i in range(heads):
        scores = parts[i * rows : (i + 1) * rows] + bias
        top = jnp.max(scores, axis=1, keepdims=True)
        scores = jnp.exp2(scores - top)
        totals.append(jnp.sum(scores, axis=1, keepdims=True))
        sums.append((top, totals[-1]))
        weights.append(scores.astype(BF16))
    mixed = mm(join(weights, 0), value)
    out = mixed[:rows] / totals[0]
    for i in range(1, heads):
        out = jnp.where(masks[i], mixed[i * rows : (i + 1) * rows] / totals[i], out)
    return out, sums


def narrow_kernel(job, layout, size, sizes, *refs):
    query_flag, key_flag, rows, keys, key_row, value_row, query_row = job
    key_refs, value_refs, query_refs = ([refs[i] for i in part] for part in layout)
    count = len(key_refs)
    tiles = [f[...].astype(F32) for f in refs[:count]]
    outs, (k_all, v_all, bias) = refs[-3 - len(query_refs) : -3], refs[-3:]
    for held, group, row in ((k_all, key_refs, key_row), (v_all, value_refs, value_row)):
        for j, ref in enumerate(group):
            held[j * keys : (j + 1) * keys, :] = ref[row : row + keys, :]
    for a, query in enumerate(query_refs):
        if query_flag is not None:
            times = column(flag_row(tiles[a], query_flag, *sizes))
        for b in range(count):
            line = flag_row(tiles[b], key_flag, *sizes)
            if query_flag is not None:
                piece = near_times(times, line)
            else:
                mask = jnp.broadcast_to(line, (rows, keys)) > 0.5
                if a == b:
                    mask = mask | (
                        lax.broadcasted_iota(jnp.int32, (rows, keys), 0)
                        == lax.broadcasted_iota(jnp.int32, (rows, keys), 1)
                    )
                piece = bias_of(mask)
            bias[:, b * keys : (b + 1) * keys] = piece
        for start in range(0, k_all.shape[1], LANES):
            lanes = slice(start, start + LANES)
            mixed, _ = attend_pair(
                query[query_row : query_row + rows, lanes],
                k_all[:, lanes],
                v_all[:, lanes],
                bias[...],
                size**-0.5 * LOG2E,
                size,
            )
            outs[a][:, lanes] = mixed.astype(BF16)


def narrow_attention(flags, keys, values, queries, job, sizes, size):
    operands, layout = list(flags), []
    for group in (keys, values, queries):
        indices = []
        for array in group:
            known = [i for i, operand in enumerate(operands) if operand is array]
            indices.append(known[0] if known else len(operands))
            if not known:
                operands.append(array)
        layout.append(indices)
    rows, all_keys, width = job[2], len(keys) * job[3], keys[0].shape[1]
    work = len(queries) * rows * all_keys * width
    return call(
        functools.partial(narrow_kernel, job, layout, size, sizes),
        operands,
        [shape(rows, width)] * len(queries),
        [
            pltpu.VMEM((all_keys, width), BF16),
            pltpu.VMEM((all_keys, width), BF16),
            pltpu.VMEM((rows, all_keys), F32),
        ],
        (8 * work, work // size),
    )


def stat_rows(width, size):
    return -(-3 * (width // size) // TILE) * TILE


def stat_layout(rows, width, size):
    total = stat_rows(width, size)
    beside = 2 if width >= 2 * rows else 1
    return total // beside, beside


def half_kernel(count, size, sizes, *refs):
    tiles, packs = [f[...].astype(F32) for f in refs[:count]], refs[count : 2 * count]
    outs, (k_all, v_all) = refs[2 * count : 3 * count], refs[3 * count :]
    keys, rows = sizes
    width, near = k_all.shape[1], count // 2
    for j in range(near):
        k_all[j * keys : (j + 1) * keys, :] = packs[j][0:keys, :]
        v_all[j * keys : (j + 1) * keys, :] = packs[j][keys : 2 * keys, :]
    times = join([flag_row(tiles[j], TIME, *sizes) for j in range(near)], 1)
    lane = lax.broadcasted_iota(jnp.int32, (1, LANES), 1)
    heads, per = width // size, LANES // size
    for a in range(count):
        first = 2 * keys if a < near else 0
        bias = near_times(column(flag_row(tiles[a], AUDIO_TIME, *sizes)), times)
        stats = jnp.zeros((rows, LANES), F32)
        for start in range(0, width, LANES):
            lanes = slice(start, start + LANES)
            mixed, sums = attend_pair(
                packs[a][first : first + rows, lanes],
                k_all[:, lanes],
                v_all[:, lanes],
                bias,
                size**-0.5 * LOG2E,
                size,
            )
            outs[a][0:rows, lanes] = mixed.astype(BF16)
            for i, (top, total) in enumerate(sums):
                rest = top + jnp.log2(total)
                for term in range(3):
                    rounded = rest.astype(BF16).astype(F32)
                    at = term * heads + start // LANES * per + i
                    stats = jnp.where(lane == at, rounded, stats)
                    rest = rest - rounded
        below, beside = stat_layout(rows, width, size)
        turned = stats.T
        pieces = [turned[i * below : (i + 1) * below, :] for i in range(beside)]
        gap = width - beside * rows
        if gap:
            pieces.append(jnp.zeros((below, gap), F32))
        outs[a][rows:, :] = join(pieces, 1).astype(BF16)


def half_attention(flags, packs, sizes, size):
    count, width = len(packs), packs[0].shape[1]
    keys, rows = sizes
    work = count * rows * (count // 2) * keys * width
    return call(
        functools.partial(half_kernel, count, size, sizes),
        [*flags, *packs],
        [shape(rows + stat_layout(rows, width, size)[0], width)] * count,
        [pltpu.VMEM((count // 2 * keys, width), BF16)] * 2,
        (8 * work, work // size),
    )


def merge_kernel(count, size, *refs):
    parts, outs = refs[:count], refs[count:]
    rows, width = outs[0].shape
    heads, per = width // size, LANES // size
    lane = lax.broadcasted_iota(jnp.int32, (1, LANES), 1)
    for c, out in enumerate(outs):
        pair = parts[c], parts[c + count // 2]
        sums = []
        for part in pair:
            below, beside = stat_layout(rows, width, size)
            tile = part[rows : rows + below, :].astype(F32)
            tile = join([tile[:, i * rows : (i + 1) * rows] for i in range(beside)], 0)
            filler = jnp.zeros((LANES - tile.shape[0], rows), F32)
            tile = join([tile, filler], 0).T
            sums.append(
                [
                    tile[:, h : h + 1]
                    + tile[:, heads + h : heads + h + 1]
                    + tile[:, 2 * heads + h : 2 * heads + h + 1]
                    for h in range(heads)
                ]
            )
        for start in range(0, width, LANES):
            lanes = slice(start, start + LANES)
            shares = []
            for i in range(per):
                one, two = (s[start // LANES * per + i] for s in sums)
                top = jnp.maximum(one, two)
                one, two = jnp.exp2(one - top), jnp.exp2(two - top)
                total = one + two
                one, two = one / total, two / total
                if shares:
                    one = jnp.where(lane >= i * size, one, shares[0])
                    two = jnp.where(lane >= i * size, two, shares[1])
                shares = [one, two]
            mixed = shares[0] * pair[0][0:rows, lanes].astype(F32)
            mixed = mixed + shares[1] * pair[1][0:rows, lanes].astype(F32)
            out[:, lanes] = mixed.astype(BF16)


def merge_halves(parts, rows, size):
    count, width = len(parts), parts[0].shape[1]
    return call(
        functools.partial(merge_kernel, count, size),
        parts,
        [shape(rows, width)] * (count // 2),
        [],
        (0, 0),
    )


def project_kernel(places, groups, with_before, *refs):
    out, refs = refs[-1], refs[:-1]
    before, refs = (refs[-1], refs[:-1]) if with_before else (None, refs)
    weights, parts = refs[len(refs) - len(groups) :], refs[: len(refs) - len(groups)]
    me, owner = lax.axis_index(SEQ), lax.axis_index(STREAM)
    _, width = out.shape[1:]
    for i, place in enumerate(places):
        columns = pl.ds(pl.multiple_of((owner ^ place) * width, width), width)
        total = before[place] if with_before else None
        for (indices, lanes), weight in zip(groups, weights):
            for j, index in enumerate(indices):
                at = ((me ^ j) & (len(indices) - 1)) * lanes
                term = mm(parts[index][...], weight[pl.ds(pl.multiple_of(at, lanes), lanes), columns])
                total = term if total is None else total + term
        out[i] = total.astype(out.dtype)


def project(places, groups, weights, rows, columns, dtype, before=None):
    parts, layout = [], []
    for members in groups:
        layout.append(([len(parts) + i for i in range(len(members))], members[0].shape[1]))
        parts += members
    depth = sum(w.shape[0] for w in weights)
    return call(
        functools.partial(project_kernel, places, layout, before is not None),
        [*parts, *weights, *([] if before is None else [before])],
        [shape(len(places), rows, columns, dtype=dtype)],
        [],
        (2 * rows * depth * columns * len(places), 0),
    )[0]


def collect_kernel(layout, *refs):
    out = refs[-1]
    for k, entries in enumerate(layout):
        total = functools.reduce(jnp.add, [refs[i][at].astype(F32) for i, at in entries])
        if len(out.shape) == 2:
            out[...] = total.astype(BF16)
        else:
            out[k] = total.astype(BF16)


def collect(sums, final=False):
    operands, layout = [], []
    for terms in sums:
        entries = []
        for array, at in terms:
            known = [i for i, operand in enumerate(operands) if operand is array]
            entries.append((known[0] if known else len(operands), at))
            if not known:
                operands.append(array)
        layout.append(entries)
    block = operands[0].shape[1:]
    out = shape(*block) if final else shape(len(sums), *block)
    return call(functools.partial(collect_kernel, layout), operands, [out], [], (0, 0))[0]


def scatter_sum(terms, count, one_by_one):
    half = count // 2
    if one_by_one:
        parts = {}
        for i in reversed(range(half)):
            arrived = swap(terms([2 * i + 1], BF16), STREAM, count, 1)
            parts[i] = [(terms([2 * i], F32), 0), (arrived, 0)]
    else:
        arrived = swap(terms(list(range(1, count, 2)), BF16), STREAM, count, 1)
        kept = terms(list(range(0, count, 2)), F32)
        parts = {i: [(kept, i), (arrived, i)] for i in range(half)}
    distance = 2
    while distance < count:
        leaving = [i for i in sorted(parts) if 2 * i & distance]
        sent = collect([parts.pop(i) for i in leaving])
        arrived = swap(sent, STREAM, count, distance)
        for k, i in enumerate(sorted(parts)):
            parts[i].append((arrived, k))
        distance *= 2
    return collect([parts[0]], True)


def shards(
    count,
    streams,
    video_query,
    video_key,
    video_value,
    video_keep,
    video_blocks,
    video_time,
    audio_query,
    audio_key,
    audio_value,
    audio_keep,
    audio_time,
    video_cross_query,
    audio_cross_key,
    audio_cross_value,
    audio_cross_query,
    video_cross_key,
    video_cross_value,
    video_out_w,
    video_cross_w,
    audio_out_w,
    audio_cross_w,
):
    rows, audio_rows = video_query.shape[0], audio_query.shape[0]
    sizes = rows, audio_rows
    size = audio_cross_w.shape[1] // HA
    narrow = audio_query.shape[1]
    by_heads = (video_query.shape[1] // BLOCK) % count == 0 and (narrow // LANES) % count == 0
    every, near = range(count), range(count // 2)

    heard_keys = gather_pairs(audio_cross_key, SEQ, count)
    heard_values = gather_pairs(audio_cross_value, SEQ, count)
    flags = flag_tile(video_keep, video_time, audio_keep, audio_time)
    if by_heads:
        (packs,) = pack([(below(video_query, video_key, video_value), every, count)])
        packs = exchange(packs, SEQ, count)
        flags = exchange([flags] * count, SEQ, count)
        crossed, questions, alone = pack(
            [
                (below(video_cross_key, video_cross_value, audio_cross_query), near, count // 2),
                (below(audio_cross_query), range(count // 2, count), count // 2),
                (below(audio_key, audio_value, audio_query), every, count),
            ],
        )
        crossed = exchange([*crossed, *questions], SEQ, count)
        alone = exchange(alone, SEQ, count)
    else:
        ((packs,),) = pack([(below(video_key, video_value), [0], 1)])
        packs = gather_pairs(packs, SEQ, count)
        flags = gather_pairs(flags, SEQ, count)
        (crossed,), (alone,) = pack(
            [
                (below(video_cross_key, video_cross_value), [0], 1),
                (below(audio_key, audio_value), [0], 1),
            ],
        )
        crossed = gather_pairs(crossed, SEQ, count)
        alone = gather_pairs(alone, SEQ, count)
    staged = pack(
        [(below(w), [0], 1) for w in (video_out_w, video_cross_w, audio_out_w, audio_cross_w)],
    )
    (video_out_w,), (video_cross_w,), (audio_out_w,), (audio_cross_w,) = staged

    def video_attention(chosen, own=None):
        return video_self_attention(video_blocks, flags, packs, chosen, rows, audio_rows, own)

    if by_heads:
        far = video_attention(list(every)[count // 2 :])
        close = video_attention(list(near))
        video_self = exchange([*close, *far], SEQ, count)
    else:
        video_self = video_attention([0], video_query)

    def audio_attention(keys, values, queries, *job):
        return narrow_attention(flags, keys, values, queries, job, sizes, size)

    video_cross = audio_attention(
        heard_keys,
        heard_values,
        [video_cross_query],
        *(TIME, AUDIO_TIME, rows, audio_rows, 0, 0, 0),
    )
    if by_heads:
        audio_cross = half_attention(flags, crossed, sizes, size)
        audio_cross = exchange(audio_cross, SEQ, count)
        audio_self = audio_attention(
            *(alone, alone, alone),
            *(None, AUDIO_KEEP, audio_rows, audio_rows, 0, audio_rows, 2 * audio_rows),
        )
        audio_self = exchange(audio_self, SEQ, count)
        audio_cross = merge_halves(audio_cross, audio_rows, size)
    else:
        audio_cross = audio_attention(
            *(crossed, crossed, [audio_cross_query]),
            *(AUDIO_TIME, TIME, audio_rows, rows, 0, rows, 0),
        )
        audio_self = audio_attention(
            *(alone, alone, [audio_query]),
            *(None, AUDIO_KEEP, audio_rows, audio_rows, 0, audio_rows, 0),
        )

    def terms(groups, weights, rows, before=None):
        columns = weights[0].shape[1] // streams
        return lambda places, dtype: project(places, groups, weights, rows, columns, dtype, before)

    video_update = scatter_sum(
        terms([video_self, video_cross], [video_out_w, video_cross_w], rows), streams, True
    )
    early = terms([audio_cross], [audio_cross_w], audio_rows)
    early = early(list(range(streams)), F32)
    audio_update = scatter_sum(terms([audio_self], [audio_out_w], audio_rows, early), streams, True)
    return video_update, audio_update


def solution(mesh):
    tokens = P((DP, SEQ))
    matrix = P((DP, SEQ), STREAM)
    weight = P(STREAM, None)
    count, streams = mesh.shape[SEQ], mesh.shape[STREAM]

    def body(*args):
        return shards(count, streams, *args)

    return jax.shard_map(
        body,
        mesh=mesh,
        in_specs=(
            matrix,
            matrix,
            matrix,
            tokens,
            P(DP, None),
            tokens,
            matrix,
            matrix,
            matrix,
            tokens,
            tokens,
            matrix,
            matrix,
            matrix,
            matrix,
            matrix,
            matrix,
            weight,
            weight,
            weight,
            weight,
        ),
        out_specs=(matrix, matrix),
        check_vma=False,
    )
```
